512 devices in a mesh: dp: 8 (over z_hi, core), fsdp: 16 (over z_lo, y), tp: 4 (over x).
Axes of the slice: x: 4, y: 8, z: 8 (z_hi: 4, z_lo: 2; z = z_hi * 2 + z_lo), core: 2. Of those that a mesh axis runs over, the one named last changes fastest.
Arguments:
- layer_input: bfloat16 [65536, 4096], P(('dp', 'fsdp'), 'tp'), may hold values from -24 to 24
- value_grad: bfloat16 [65536, 2048], P(('dp', 'fsdp'), 'tp'), may hold values from -6 to 6
- residual_grad: bfloat16 [65536, 4096], P(('dp', 'fsdp'), 'tp'), may hold values from -6 to 6
- value_weight: bfloat16 [4096, 2048], P(('tp', 'fsdp')), may hold values from -0.125 to 0.125
- owner: int32 [65536, 1], P(('dp', 'fsdp')), may hold values from 0 to 15; in each aligned block of 512 rows (0 to 511, 512 to 1023, ...) at most 64 rows name the same one
- key_row: int32 [65536], P(('dp', 'fsdp')), may hold values from 0 to 255
Outputs:
- weight_grad: float32 [4096, 2048], P(('tp', 'fsdp'))
- key_grad: float32 [4096, 4096], P('fsdp', 'tp')
The draws below stay inside these ranges and needn't reach their ends.
Inputs may be any that keep to these rules, and one draw needn't show every extreme that they name: Among the 512 tokens of one device (aligned blocks of rows) at most 64 name the same owner, and that bound is reached.
All inputs are finite; a program needn't handle non-finite values.
Results may differ from the reference program's by a relative error of at most 0.0029.
Values may be sent and summed in bfloat16 or wider, within the bound.
A program may use at most 64 MiB of HBM per device.

```python
import math
import jax
import jax.numpy as jnp
import numpy as np
from jax import lax

D = 4096
HW = 2048
TOK_DEV = 512
KEY_DEV = 256
CAP = 64
TOKENS = 65536
NKEYS = 4096
N_FSDP = 16


def place_ends(drawn, rng, smallest, largest):
    longest = drawn.shape.index(max(drawn.shape))
    spots = []
    for shift in (0, 1):
        where = [jax.random.randint(jax.random.fold_in(rng, axis), (), 0, length) for axis, length in enumerate(drawn.shape)]
        where[longest] = (where[longest] + shift) % drawn.shape[longest]
        spots.append(tuple(where))
    return drawn.at[spots[0]].set(smallest).at[spots[1]].set(largest)


def with_spikes(array, stream_key, source, target, shards_of, factor):
    owner, partner = [(jnp.arange(array.shape[axis_at]) // (array.shape[axis_at] // shards_of)).reshape([-1 if axis == axis_at else 1 for axis in range(array.ndim)]) for axis_at in (source, target)]
    chosen = jax.random.permutation(stream_key, shards_of)[partner]
    strong = (owner == chosen) | (owner == (partner + shards_of // 2) % shards_of)
    return jnp.where(strong, factor * array, array)


def block_levels(rng, shape, shards, least, largest):
    def one(position, shards_of):
        draws = jax.random.uniform(jax.random.fold_in(jax.random.fold_in(rng, 6), position), (shards_of,), jnp.float32, least / len(shards), largest / len(shards))
        return jnp.repeat(jnp.exp(draws), shape[position] // shards_of).reshape((-1,) + (1,) * (len(shape) - position - 1))

    level = one(*shards[0])
    for cut in shards[1:]:
        level = level * one(*cut)
    return level


def deal_out(key, own, number, rows, count, top, bound, lean):
    ranking = jax.random.permutation(key, count)
    heavy_load, common = shares(count, rows * top, bound, lean, True), shares(count, rows * top, bound, lean, False)
    places = jnp.arange(count)

    def named(tallies, offset_by):
        used = int((tallies > 0).sum())
        fixed = max(1, used // 4)
        passed = fixed + (places - fixed + offset_by * (used - fixed)) % max(1, count - fixed)
        return jnp.zeros((count,), jnp.int32).at[ranking[jnp.where(places < fixed, places, passed)]].set(jnp.asarray(tallies, jnp.int32))

    tallies = jnp.where(number % 4 == 0, named(heavy_load, number // 4), named(common, number - number // 4 - 1))
    mixed = jax.random.permutation(jax.random.fold_in(own, 3), count)
    giver, taker = mixed[0:count // 2 * 2:2], mixed[1:count // 2 * 2:2]
    margin = jnp.minimum(tallies[giver] - 1, bound - tallies[taker]) // 2
    margin = jnp.where((giver == ranking[0]) | (taker == ranking[0]) | (tallies[taker] == 0), 0, jnp.maximum(margin, 0))
    passed = jax.random.randint(jax.random.fold_in(own, 4), (count // 2,), 0, 1 << 20) % (margin + 1)
    tallies = tallies.at[giver].add(-passed).at[taker].add(passed)
    labels = jnp.searchsorted(jnp.cumsum(tallies), jnp.arange(rows * top), side="right").astype(jnp.int32)
    grid = labels.reshape(top, rows).T
    grid = grid[jax.random.permutation(jax.random.fold_in(own, 1), rows)]
    offset_by = jax.random.randint(jax.random.fold_in(own, 2), (rows, 1), 0, top)
    return jnp.take_along_axis(grid, (jnp.arange(top)[None, :] + offset_by) % top, axis=1)


def shares(amount, total, most, slope, full):
    loads = [(1 << 20) // math.isqrt(grade ** slope) + 1 for grade in range(1, amount + 1)]
    largest = most if full else min(most, max(-(-total // amount), total * loads[0] // sum(loads)))
    least = 1 if total - largest >= amount - 1 else 0
    holding, surplus = [largest] + [least] * (amount - 1), total - largest - least * (amount - 1)
    while surplus > 0:
        movable = [i for i in range(1, amount) if holding[i] < largest] or [i for i in range(1, amount) if holding[i] < most]
        pool, remaining = sum([loads[i] for i in movable]), surplus
        for i in movable:
            extra = min(most - holding[i], max(1, remaining * loads[i] // pool), surplus)
            holding[i] = holding[i] + extra
            surplus = surplus - extra
    return np.array(holding)


def gaussian(own_key, dims, scale, reach, pieces=(), held_as=jnp.bfloat16):
    array = jax.random.normal(own_key, dims, jnp.float32) * scale
    if len(pieces) > 0:
        array = block_levels(own_key, dims, pieces, -0.22, 0.18) * array
    return jnp.clip(array, min=-reach, max=reach).astype(held_as)


def noise_with(rng, extent, width, limit, split, heavy, dtype=jnp.bfloat16):
    result = width * jax.random.normal(rng, extent, jnp.float32)
    if split:
        result = result * block_levels(rng, extent, split, -0.22, 0.18)
    return jnp.clip(with_spikes(result, jax.random.fold_in(rng, 3), *heavy), -limit, limit).astype(dtype)


def setup_inputs(seed: int = 0) -> dict:
    seeds = jax.random.split(jax.random.key(seed), 7)
    layer_input = noise_with(seeds[0], (TOKENS, D), 1.0, 24.0, ((0, 128), (1, 4)), (0, 1, 128, 5.5))
    value_grad = gaussian(seeds[1], (TOKENS, HW), 1.0, 6.0, ((0, 128), (1, 4)))
    residual_grad = gaussian(seeds[2], (TOKENS, D), 1.0, 6.0, ((0, 128), (1, 4)))
    value_weight = gaussian(seeds[3], (D, HW), HW ** -0.5, 0.125, ((0, 64),))
    owner_keys = jax.random.split(jax.random.fold_in(seeds[4], 1), TOKENS // TOK_DEV)
    owner_turns = jax.random.permutation(jax.random.fold_in(seeds[4], 3), TOKENS // TOK_DEV)
    owner = jax.vmap(lambda own, number: deal_out(jax.random.fold_in(seeds[4], 2), own, number, TOK_DEV, N_FSDP, 1, CAP, 2))(owner_keys, owner_turns).reshape((TOKENS, 1))
    key_row = place_ends(jax.random.randint(seeds[5], (TOKENS,), 0, KEY_DEV), jax.random.fold_in(seeds[5], 1), 0, KEY_DEV - 1).astype(jnp.int32)
    return dict(layer_input=layer_input, value_grad=value_grad, residual_grad=residual_grad, value_weight=value_weight, owner=owner, key_row=key_row)


def reference(layer_input, value_grad, residual_grad, value_weight, owner, key_row):
    blocks = TOKENS // TOK_DEV
    inputs = layer_input.reshape(blocks, TOK_DEV, D)
    grads = value_grad.reshape(blocks, TOK_DEV, HW)
    residual = residual_grad.reshape(blocks, TOK_DEV, D)
    keys = (owner[:, 0] * KEY_DEV + key_row).astype(jnp.int32).reshape(blocks, TOK_DEV)

    def step(carry, items):
        weight_acc, table = carry
        block_in, block_grad, block_res, block_keys = items
        partial_value = jnp.dot(block_in.T, block_grad, preferred_element_type=jnp.float32).astype(jnp.bfloat16)
        partial_value = lax.optimization_barrier(partial_value)
        weight_acc = weight_acc + partial_value.astype(jnp.float32)
        back = jnp.dot(block_grad, value_weight.T, preferred_element_type=jnp.float32)
        input_grad = (block_res.astype(jnp.float32) + back).astype(jnp.bfloat16)
        table = table + jax.ops.segment_sum(input_grad.astype(jnp.float32), block_keys, NKEYS)
        return (weight_acc, table), None

    start = (jnp.zeros((D, HW), jnp.float32), jnp.zeros((NKEYS, D), jnp.float32))
    (weight_grad, key_grad), _ = lax.scan(step, start, (inputs, grads, residual, keys))
    return weight_grad, key_grad
```

```python
import jax
import jax.numpy as jnp
from jax import lax
from jax.experimental import pallas as pl
from jax.experimental.pallas import tpu as pltpu
from jax.sharding import PartitionSpec as P

MESH = pl.DeviceIdType.MESH
BF, F32 = jnp.bfloat16, jnp.float32
NX, NY, NZ, NH = 4, 8, 8, 4
TOK, FEAT, HEADS, WIDTH = 512, 512, 512, 2048
SLOTS, KEYS, ROWS, COLS = 64, 256, 64, 256
HALF = TOK // 2


def dot(a, b, dims):
    return lax.dot_general(a, b, (dims, ((), ())), preferred_element_type=F32)


def kernel(
    li_ref, vgr_ref, res_ref, wsh_ref, own_ref, key_ref,
    wout, kout,
    vg, li2, res_p, own_p, key_p, w, wp, wr, ws, yr, wf, acc, igb, pk, km, kr, kmr, table, tb, zr, kf,
    loc, p_s, p_r, x_s, x_r, v_s, v_r, wy_s, wy_r, wz_s, wz_r,
    a_s, a_r, k_s, k_r, m_s, m_r, b_s, b_r, z_s, z_r, d_s, d_r, e_s, e_r, f_s, f_r, g_s, g_r,
):
    dp, fs, x = lax.axis_index("dp"), lax.axis_index("fsdp"), lax.axis_index("tp")
    zh, c, zl, y = dp // 2, dp % 2, fs // NY, fs % NY
    z = zh * 2 + zl
    near = zl == c
    far = zl != c

    def at(x_=x, y_=y, z_=z, c_=c):
        return ((z_ // 2) * 2 + c_, (z_ % 2) * NY + y_, x_)

    partner = at(c_=1 - c)
    right, left = (x + 1) % NX, (x + NX - 1) % NX
    ended = []

    def send(src, dst, ss, rs, to, later=True):
        pltpu.make_async_remote_copy(
            src_ref=src, dst_ref=dst, send_sem=ss, recv_sem=rs, device_id=to, device_id_type=MESH
        ).start()
        if later:
            ended.append((src, ss))

    def got(dst, rs):
        pltpu.make_async_copy(dst, dst, rs).wait()

    def cols(i):
        return pl.ds(pl.multiple_of(i * HEADS, HEADS), HEADS)

    def mine(i):
        return pl.ds(pl.multiple_of(i * FEAT, FEAT), FEAT)

    def shard(i, start=0, size=ROWS):
        return pl.ds(pl.multiple_of(i * ROWS + start, 32), size)

    barrier = pltpu.get_barrier_semaphore()
    peers = [partner, at(x_=right), at(x_=left)]
    peers += [at(y_=(y + d) % NY) for d in range(1, NY)] + [at(z_=(z + d) % NZ) for d in range(1, NZ)]
    for peer in peers:
        pl.semaphore_signal(barrier, inc=1, device_id=peer, device_id_type=MESH)
    pl.semaphore_wait(barrier, len(peers))

    top, low = pl.ds(0, HALF), pl.ds(HALF, HALF)
    send(vgr_ref.at[top], vg.at[0, top, cols(x)], x_s.at[0], x_r.at[0], at(x_=right))
    send(vgr_ref.at[low], vg.at[0, low, cols(x)], x_s.at[2], x_r.at[2], at(x_=left))
    send(vgr_ref.at[low], vg.at[0, low, cols(x)], x_s.at[1], x_r.at[1], at(x_=right))
    send(vgr_ref.at[top], vg.at[0, top, cols(x)], x_s.at[3], x_r.at[3], at(x_=left))

    up, down = at(z_=(z + 1) % NZ), at(z_=(z + NZ - 1) % NZ)
    after, before = at(y_=(y + 1) % NY), at(y_=(y + NY - 1) % NY)

    @pl.when(near)
    def _():
        send(wsh_ref, w.at[shard(y)], wy_s.at[0], wy_r.at[0], after, False)
        send(wsh_ref, w.at[shard(y)], wy_s.at[4], wy_r.at[4], before, False)
        send(wsh_ref.at[pl.ds(0, 32)], w.at[shard(y, 0, 32)], wz_s.at[0], wz_r.at[0], up, False)
        send(wsh_ref.at[pl.ds(32, 32)], w.at[shard(y, 32, 32)], wz_s.at[1], wz_r.at[1], down, False)
        pltpu.make_async_copy(wsh_ref, w.at[shard(y)], loc.at[2]).start()

    send(vgr_ref, vg.at[1, :, cols(x)], v_s.at[0], v_r.at[0], partner)
    send(li_ref.at[:, mine(1 - c)], li2.at[1], p_s.at[0], p_r.at[0], partner)
    send(own_ref, own_p, p_s.at[1], p_r.at[1], partner)
    send(key_ref, key_p, p_s.at[2], p_r.at[2], partner)
    send(res_ref.at[:, mine(1 - c)], res_p, p_s.at[3], p_r.at[3], partner)
    own_vg = pltpu.make_async_copy(vgr_ref, vg.at[0, :, cols(x)], loc.at[0])
    own_vg.start()
    own_li = pltpu.make_async_copy(li_ref.at[:, mine(c)], li2.at[0], loc.at[1])
    own_li.start()

    def weights(k):
        plus, minus = (y + NY - k) % NY, (y + k) % NY
        got(w.at[shard(plus)], wy_r.at[k - 1])
        part = (0, 32) if k == 3 else (0, ROWS)
        send(w.at[shard(plus, *part)], w.at[shard(plus, *part)], wy_s.at[k], wy_r.at[k], after, False)
        send(w.at[shard(plus)], w.at[shard(plus)], wz_s.at[1 + k], wz_r.at[1 + k], down, False)
        got(w.at[shard(minus)], wy_r.at[3 + k])
        part = (32, 32) if k == 3 else (0, ROWS)
        send(w.at[shard(minus, *part)], w.at[shard(minus, *part)], wy_s.at[4 + k], wy_r.at[4 + k], before, False)
        send(w.at[shard(minus)], w.at[shard(minus)], wz_s.at[4 + k], wz_r.at[4 + k], up, False)

    def places(owner):
        hot = (lax.broadcasted_iota(jnp.int32, (16, TOK), 0) == owner).astype(F32)
        order = lax.broadcasted_iota(jnp.int32, (TOK, TOK), 0) <= lax.broadcasted_iota(jnp.int32, (TOK, TOK), 1)
        count = dot(hot.astype(BF), order.astype(F32).astype(BF), ((1,), (0,)))
        rank = jnp.sum(count * hot, axis=0, keepdims=True) - 1.0
        return owner * SLOTS + rank.astype(jnp.int32)

    slot = [places(own_ref[...]), None]

    @pl.when(near)
    def _():
        weights(1)

    got(vg.at[0, top, cols(left)], x_r.at[0])
    send(vg.at[0, top, cols(left)], vg.at[0, top, cols(left)], x_s.at[4], x_r.at[4], at(x_=right))
    send(vg.at[0, top, cols(left)], vg.at[1, top, cols(left)], v_s.at[1], v_r.at[1], partner)
    got(vg.at[0, low, cols(right)], x_r.at[2])
    send(vg.at[0, low, cols(right)], vg.at[0, low, cols(right)], x_s.at[5], x_r.at[5], at(x_=left))
    send(vg.at[0, low, cols(right)], vg.at[1, low, cols(right)], v_s.at[2], v_r.at[2], partner)

    @pl.when(near)
    def _():
        weights(2)

    def weight_tile(q):
        total = None
        for b in range(2):
            part = dot(li2[b], vg[b, :, cols(q)], ((0,), (0,))).astype(BF).astype(F32)
            total = part if total is None else total + part
        total = total.astype(BF)
        wp[2 * q] = total[:, :COLS]
        wp[2 * q + 1] = total[:, COLS:]

    own_vg.wait()
    own_li.wait()
    got(li2.at[1], p_r.at[0])
    got(vg.at[1, :, cols(x)], v_r.at[0])
    weight_tile(x)

    @pl.when(near)
    def _():
        weights(3)

    got(vg.at[0, low, cols(left)], x_r.at[1])
    send(vg.at[0, low, cols(left)], vg.at[1, low, cols(left)], v_s.at[3], v_r.at[3], partner)
    got(vg.at[0, top, cols(right)], x_r.at[3])
    send(vg.at[0, top, cols(right)], vg.at[1, top, cols(right)], v_s.at[4], v_r.at[4], partner)

    opposite = (y + 4) % NY

    @pl.when(near)
    def _():
        got(w.at[shard(opposite, 0, 32)], wy_r.at[3])
        send(w.at[shard(opposite, 0, 32)], w.at[shard(opposite, 0, 32)], wz_s.at[8], wz_r.at[8], up, False)
        got(w.at[shard(opposite, 32, 32)], wy_r.at[7])
        send(w.at[shard(opposite, 32, 32)], w.at[shard(opposite, 32, 32)], wz_s.at[9], wz_r.at[9], down, False)

    got(own_p, p_r.at[1])
    got(key_p, p_r.at[2])
    slot[1] = places(own_p[...])

    got(vg.at[1, top, cols(left)], v_r.at[1])
    got(vg.at[1, low, cols(left)], v_r.at[3])
    weight_tile(left)

    across = (x + 2) % NX
    got(vg.at[0, top, cols(across)], x_r.at[4])
    send(vg.at[0, top, cols(across)], vg.at[1, top, cols(across)], v_s.at[5], v_r.at[5], partner)
    got(vg.at[0, low, cols(across)], x_r.at[5])
    send(vg.at[0, low, cols(across)], vg.at[1, low, cols(across)], v_s.at[6], v_r.at[6], partner)

    got(vg.at[1, low, cols(right)], v_r.at[2])
    got(vg.at[1, top, cols(right)], v_r.at[4])
    weight_tile(right)

    @pl.when(near)
    def _():
        pltpu.make_async_copy(wsh_ref, w.at[shard(y)], loc.at[2]).wait()

    @pl.when(far)
    def _():
        got(w.at[shard(y, 0, 32)], wz_r.at[0])
        got(w.at[shard(y, 32, 32)], wz_r.at[1])
        for k in range(1, 4):
            got(w.at[shard((y + NY - k) % NY)], wz_r.at[1 + k])
            got(w.at[shard((y + k) % NY)], wz_r.at[4 + k])
        got(w.at[shard(opposite, 0, 32)], wz_r.at[8])
        got(w.at[shard(opposite, 32, 32)], wz_r.at[9])

    got(res_p, p_r.at[3])
    acc[0] = res_ref[:, mine(c)].astype(F32)
    acc[1] = res_p[...].astype(F32)

    def back_tile(q):
        for b in range(2):
            acc[b] += dot(vg[b, :, cols(q)], w[:, cols(q)], ((1,), (1,)))

    back_tile(x)
    back_tile(left)
    back_tile(right)
    got(vg.at[1, top, cols(across)], v_r.at[5])
    got(vg.at[1, low, cols(across)], v_r.at[6])
    back_tile(across)
    igb[...] = acc[...].astype(BF)

    line = lax.broadcasted_iota(jnp.int32, (2 * SLOTS, 1), 0)
    keys = [jnp.broadcast_to((ref[...] + 1).astype(F32), (8, TOK)).astype(BF) for ref in (key_ref, key_p)]

    def pack(d):
        to = (y + d) % NY
        wanted = (line // SLOTS) * (NY * SLOTS) + to * SLOTS + line % SLOTS
        for b in range(2):
            pick = (wanted == slot[b]).astype(F32).astype(BF)
            pk[d, pl.ds(b * 2 * SLOTS, 2 * SLOTS)] = dot(pick, igb[b], ((1,), (0,))).astype(BF)
            km[d, :, pl.ds(b * 2 * SLOTS, 2 * SLOTS)] = dot(keys[b], pick, ((1,), (1,)))
        if d > 0:
            send(pk.at[d], kr.at[d], k_s.at[d], k_r.at[d], at(y_=to))
            send(km.at[d], kmr.at[d], m_s.at[d], m_r.at[d], at(y_=to))

    for d in (4, 3, 5, 2, 6, 1, 7, 0):
        pack(d)

    weight_tile(across)
    for d in (4, 3, 5, 2, 6, 1, 7):
        to = (z + d) % NZ
        send(wp.at[to], wr.at[d], a_s.at[d], a_r.at[d], at(z_=to))

    lane = lax.broadcasted_iota(jnp.int32, (1, 4 * SLOTS), 1)
    offset = ((lane // SLOTS) % 2) * KEYS - 1

    def tally(d, rows, marks):
        named = marks[d, 0:1, :].astype(jnp.int32)
        number = jnp.where(named > 0, named + offset, -1)
        hit = (lax.broadcasted_iota(jnp.int32, (2 * KEYS, 4 * SLOTS), 0) == number).astype(F32).astype(BF)
        return dot(hit, rows[d], ((1,), (0,)))

    table[...] = tally(0, pk, km)
    for d in (1, 7, 2, 6, 3, 5, 4):
        got(kr.at[d], k_r.at[d])
        got(kmr.at[d], m_r.at[d])
        table[...] += tally(d, kr, kmr)
    tb[...] = table[...].astype(BF)

    def piece(place):
        return pl.ds(pl.multiple_of(((place % 2) * NH + place // 2) * ROWS, ROWS), ROWS)

    for d in (4, 3, 5, 2, 6, 1, 7):
        to = (z + d) % NZ
        send(tb.at[piece(to)], zr.at[d], z_s.at[d], z_r.at[d], at(z_=to))

    for d in (1, 7, 2, 6, 3, 5, 4):
        got(wr.at[d], a_r.at[d])

    @pl.loop(0, NY)
    def _(i):
        rows = pl.ds(pl.multiple_of(i * ROWS, ROWS), ROWS)
        total = wp[z, rows].astype(F32)
        for d in range(1, NZ):
            total = total + wr[d, rows].astype(F32)
        ws[i] = total.astype(BF)

    for d in (4, 3, 5, 2, 6, 1, 7):
        to = (y + d) % NY
        send(ws.at[to], yr.at[d], b_s.at[d], b_r.at[d], at(y_=to))

    total = table[piece(z), :]
    for d in (1, 7, 2, 6, 3, 5, 4):
        got(zr.at[d], z_r.at[d])
        total = total + zr[d].astype(F32)
    kf[...] = total

    def block(i):
        return pl.ds(pl.multiple_of(i * ROWS, ROWS), ROWS)

    for e in (2, 1, 3):
        send(kf, kout.at[block(zh), mine(c)], d_s.at[e], d_r.at[e], at(z_=((zh + e) % NH) * 2 + zl))
    send(kf, kout.at[block(zh), mine(c)], e_s.at[0], e_r.at[0], partner)
    kout[block(zh), mine(c)] = total

    total = ws[y].astype(F32)
    for d in (1, 7, 2, 6, 3, 5, 4):
        got(yr.at[d], b_r.at[d])
        total = total + yr[d].astype(F32)
    wf[...] = total

    def strip(i):
        return pl.ds(pl.multiple_of(i * COLS, COLS), COLS)

    for e in (2, 1, 3):
        send(wf, wout.at[:, strip(z)], f_s.at[e], f_r.at[z], at(z_=((zh + e) % NH) * 2 + c))

    @pl.when(far)
    def _():
        send(wf, wout.at[:, strip(z)], f_s.at[0], f_r.at[z], at(z_=zh * 2 + c), False)

    @pl.when(near)
    def _():
        wout[:, strip(z)] = wf[...]
        send(wf, wout.at[:, strip(z)], g_s.at[0], g_r.at[0], partner, False)

    for e in (1, 3, 2):
        source = (zh + NH - e) % NH
        here = kout.at[block(source), mine(c)]
        got(here, d_r.at[e])
        send(here, here, e_s.at[e], e_r.at[e], partner)

    @pl.when(near)
    def _():
        for d in (1, 7, 2, 6, 3, 5, 4):
            here = wout.at[:, strip((z + d) % NZ)]
            got(here, f_r.at[(z + d) % NZ])
            send(here, here, g_s.at[d], g_r.at[d], partner, False)

    @pl.when(far)
    def _():
        for d in range(NZ):
            got(wout.at[:, strip((z + d) % NZ)], g_r.at[d])

    for e in range(NH):
        got(kout.at[block((zh + NH - e) % NH), mine(1 - c)], e_r.at[e])

    for src, sem in ended:
        got(src, sem)

    @pl.when(near)
    def _():
        for k in (0, 1, 2, 4, 5, 6):
            got(wsh_ref, wy_s.at[k])
        for k in (3, 7):
            got(wsh_ref.at[pl.ds(0, 32)], wy_s.at[k])
        for k in range(2, 8):
            got(wsh_ref, wz_s.at[k])
        for k in (0, 1, 8, 9):
            got(wsh_ref.at[pl.ds(0, 32)], wz_s.at[k])
        for d in range(NZ):
            got(wf, g_s.at[d])

    @pl.when(far)
    def _():
        got(wf, f_s.at[0])


def body(layer_input, value_grad, residual_grad, value_weight, owner, key_row):
    dma = pltpu.SemaphoreType.DMA
    vmem = pl.BlockSpec(memory_space=pltpu.VMEM)
    scratch = [
        pltpu.VMEM((2, TOK, WIDTH), BF),
        pltpu.VMEM((2, TOK, FEAT), BF),
        pltpu.VMEM((TOK, FEAT), BF),
        pltpu.VMEM((1, TOK), jnp.int32),
        pltpu.VMEM((1, TOK), jnp.int32),
        pltpu.VMEM((FEAT, WIDTH), BF),
        pltpu.VMEM((NZ, FEAT, COLS), BF),
        pltpu.VMEM((NZ, FEAT, COLS), BF),
        pltpu.VMEM((NY, ROWS, COLS), BF),
        pltpu.VMEM((NY, ROWS, COLS), BF),
        pltpu.VMEM((ROWS, COLS), F32),
        pltpu.VMEM((2, TOK, FEAT), F32),
        pltpu.VMEM((2, TOK, FEAT), BF),
        pltpu.VMEM((NY, 4 * SLOTS, FEAT), BF),
        pltpu.VMEM((NY, 8, 4 * SLOTS), F32),
        pltpu.VMEM((NY, 4 * SLOTS, FEAT), BF),
        pltpu.VMEM((NY, 8, 4 * SLOTS), F32),
        pltpu.VMEM((2 * KEYS, FEAT), F32),
        pltpu.VMEM((2 * KEYS, FEAT), BF),
        pltpu.VMEM((NZ, ROWS, FEAT), BF),
        pltpu.VMEM((ROWS, FEAT), F32),
        dma((3,)),
    ]
    for number in (4, 6, 7, 8, 10, 8, 8, 8, 8, 8, 4, 4):
        scratch += [dma((number,)), dma((number,))]
    scratch += [dma((4,)), dma((8,)), dma((8,)), dma((8,))]
    return pl.pallas_call(
        kernel,
        out_shape=(
            jax.ShapeDtypeStruct((ROWS, WIDTH), F32),
            jax.ShapeDtypeStruct((KEYS, 2 * FEAT), F32),
        ),
        in_specs=[vmem] * 6,
        out_specs=(vmem, vmem),
        scratch_shapes=scratch,
        compiler_params=pltpu.CompilerParams(
            collective_id=0, has_side_effects=True, vmem_limit_bytes=60 * 1024 * 1024
        ),
    )(layer_input, value_grad, residual_grad, value_weight, owner.reshape(1, TOK), key_row.reshape(1, TOK))


def solution(mesh):
    return jax.shard_map(
        body,
        mesh=mesh,
        in_specs=(
            P(("dp", "fsdp"), "tp"),
            P(("dp", "fsdp"), "tp"),
            P(("dp", "fsdp"), "tp"),
            P(("tp", "fsdp"), None),
            P(("dp", "fsdp"), None),
            P(("dp", "fsdp")),
        ),
        out_specs=(P(("tp", "fsdp"), None), P("fsdp", "tp")),
        check_vma=False,
    )
```

```python
import jax
import jax.numpy as jnp
from jax import lax
from jax.experimental import pallas as pl
from jax.experimental.pallas import tpu as pltpu
from jax.sharding import PartitionSpec as P

MESH = pl.DeviceIdType.MESH
BF, F32 = jnp.bfloat16, jnp.float32
NX, NY, NZ, NH = 4, 8, 8, 4
TOK, FEAT, HEADS, WIDTH = 512, 512, 512, 2048
SLOTS, KEYS, ROWS, COLS = 64, 256, 64, 256
HALF = TOK // 2
PART = FEAT // 2
ORDER = (4, 3, 5, 2, 6, 1, 7)


def dot(a, b, dims):
    return lax.dot_general(a, b, (dims, ((), ())), preferred_element_type=F32)


def kernel(
    li_ref, vgr_ref, res_ref, wsh_ref, own_ref, key_ref,
    wout, kout,
    vg, li2, res2, own_p, key_p, w, wp, cr, cs, cfs, cfr, ctot, ws, yr, wf, acc, igb, pk, km, kr, kmr, table, tb, zr, kb,
    loc, p_s, p_r, x_s, x_r, v_s, v_r, wy_s, wy_r, wz_s, wz_r,
    c_s, c_r, k_s, k_r, m_s, m_r, b_s, b_r, z_s, z_r, d_s, d_r, e_s, e_r, f_s, f_r, g_s, g_r,
):
    dp, fs, x = lax.axis_index("dp"), lax.axis_index("fsdp"), lax.axis_index("tp")
    zh, c, zl, y = dp // 2, dp % 2, fs // NY, fs % NY
    z = zh * 2 + zl
    near = zl == c
    far = zl != c

    def at(x_=x, y_=y, z_=z, c_=c):
        return ((z_ // 2) * 2 + c_, (z_ % 2) * NY + y_, x_)

    partner = at(c_=1 - c)
    right, left = (x + 1) % NX, (x + NX - 1) % NX
    ended = []

    def send(src, dst, ss, rs, to, later=True):
        pltpu.make_async_remote_copy(
            src_ref=src, dst_ref=dst, send_sem=ss, recv_sem=rs, device_id=to, device_id_type=MESH
        ).start()
        if later:
            ended.append((src, ss))

    def got(dst, rs):
        pltpu.make_async_copy(dst, dst, rs).wait()

    def cols(i):
        return pl.ds(pl.multiple_of(i * HEADS, HEADS), HEADS)

    def mine(i):
        return pl.ds(pl.multiple_of(i * FEAT, FEAT), FEAT)

    def half(i, h):
        return pl.ds(pl.multiple_of(i * ROWS + h * 32, 32), 32)

    def block(i):
        return pl.ds(pl.multiple_of(i * ROWS, ROWS), ROWS)

    barrier = pltpu.get_barrier_semaphore()
    peers = [partner, at(x_=right), at(x_=left)]
    peers += [at(y_=(y + d) % NY) for d in range(1, NY)] + [at(z_=(z + d) % NZ) for d in range(1, NZ)]
    for peer in peers:
        pl.semaphore_signal(barrier, inc=1, device_id=peer, device_id_type=MESH)

    own_vg = pltpu.make_async_copy(vgr_ref, vg.at[0, :, cols(x)], loc.at[0])
    own_vg.start()
    own_li = pltpu.make_async_copy(li_ref.at[:, mine(c)], li2.at[0], loc.at[1])
    own_li.start()
    own_res = pltpu.make_async_copy(res_ref.at[:, mine(c)], res2.at[0], loc.at[2])
    own_res.start()

    @pl.when(near)
    def _():
        pltpu.make_async_copy(wsh_ref, w.at[block(y)], loc.at[3]).start()

    pl.semaphore_wait(barrier, len(peers))

    up, down = at(z_=(z + 1) % NZ), at(z_=(z + NZ - 1) % NZ)
    after, before = at(y_=(y + 1) % NY), at(y_=(y + NY - 1) % NY)
    first, second = pl.ds(0, 32), pl.ds(32, 32)

    @pl.when(near)
    def _():
        for h, rows in enumerate((first, second)):
            send(wsh_ref.at[rows], w.at[half(y, h)], wy_s.at[h], wy_r.at[h], after, False)
            send(wsh_ref.at[rows], w.at[half(y, h)], wy_s.at[8 + h], wy_r.at[8 + h], before, False)
        send(wsh_ref.at[first], w.at[half(y, 0)], wz_s.at[0], wz_r.at[0], up, False)
        send(wsh_ref.at[second], w.at[half(y, 1)], wz_s.at[8], wz_r.at[8], down, False)

    top, low = pl.ds(0, HALF), pl.ds(HALF, HALF)
    send(vgr_ref.at[top], vg.at[0, top, cols(x)], x_s.at[0], x_r.at[0], at(x_=right))
    send(vgr_ref.at[low], vg.at[0, low, cols(x)], x_s.at[2], x_r.at[2], at(x_=left))
    send(vgr_ref.at[low], vg.at[0, low, cols(x)], x_s.at[1], x_r.at[1], at(x_=right))
    send(vgr_ref.at[top], vg.at[0, top, cols(x)], x_s.at[3], x_r.at[3], at(x_=left))
    send(vgr_ref, vg.at[1, :, cols(x)], v_s.at[0], v_r.at[0], partner)
    send(li_ref.at[:, mine(1 - c)], li2.at[1], p_s.at[0], p_r.at[0], partner)
    send(own_ref, own_p, p_s.at[1], p_r.at[1], partner)
    send(key_ref, key_p, p_s.at[2], p_r.at[2], partner)
    send(res_ref.at[:, mine(1 - c)], res2.at[1], p_s.at[3], p_r.at[3], partner)

    def weights(k):
        plus, minus = (y + NY - k) % NY, (y + k) % NY
        for h in range(2):
            for base, shard, onward, side, keeps in ((0, plus, after, down, 0), (8, minus, before, up, 1)):
                if k == 4 and h != keeps:
                    continue
                here = w.at[half(shard, h)]
                got(here, wy_r.at[base + 2 * (k - 1) + h])
                if k < 3 or (k == 3 and h == keeps):
                    send(here, here, wy_s.at[base + 2 * k + h], wy_r.at[base + 2 * k + h], onward, False)
                if k < 4:
                    number = (8 if base == 0 else 0) + 2 * k - 1 + h
                    send(here, here, wz_s.at[number], wz_r.at[number], side, False)
                else:
                    number = 7 if base == 0 else 15
                    send(here, here, wz_s.at[number], wz_r.at[number], up if base == 0 else down, False)

    def places(owner):
        hot = (lax.broadcasted_iota(jnp.int32, (16, TOK), 0) == owner).astype(F32)
        order = lax.broadcasted_iota(jnp.int32, (TOK, TOK), 0) <= lax.broadcasted_iota(jnp.int32, (TOK, TOK), 1)
        count = dot(hot.astype(BF), order.astype(F32).astype(BF), ((1,), (0,)))
        rank = jnp.sum(count * hot, axis=0, keepdims=True) - 1.0
        return owner * SLOTS + rank.astype(jnp.int32)

    slot = [places(own_ref[...]), None]

    @pl.when(near)
    def _():
        weights(1)

    got(vg.at[0, top, cols(left)], x_r.at[0])
    send(vg.at[0, top, cols(left)], vg.at[0, top, cols(left)], x_s.at[4], x_r.at[4], at(x_=right))
    send(vg.at[0, top, cols(left)], vg.at[1, top, cols(left)], v_s.at[1], v_r.at[1], partner)
    got(vg.at[0, low, cols(right)], x_r.at[2])
    send(vg.at[0, low, cols(right)], vg.at[0, low, cols(right)], x_s.at[5], x_r.at[5], at(x_=left))
    send(vg.at[0, low, cols(right)], vg.at[1, low, cols(right)], v_s.at[2], v_r.at[2], partner)

    @pl.when(near)
    def _():
        weights(2)

    def weight_tile(q):
        total = None
        for b in range(2):
            part = dot(li2[b], vg[b, :, cols(q)], ((0,), (0,))).astype(BF).astype(F32)
            total = part if total is None else total + part
        total = total.astype(BF)
        wp[2 * q] = total[:, :COLS]
        wp[2 * q + 1] = total[:, COLS:]

    own_vg.wait()
    own_li.wait()
    got(li2.at[1], p_r.at[0])
    got(vg.at[1, :, cols(x)], v_r.at[0])
    weight_tile(x)

    @pl.when(near)
    def _():
        weights(3)

    got(vg.at[0, low, cols(left)], x_r.at[1])
    send(vg.at[0, low, cols(left)], vg.at[1, low, cols(left)], v_s.at[3], v_r.at[3], partner)
    got(vg.at[0, top, cols(right)], x_r.at[3])
    send(vg.at[0, top, cols(right)], vg.at[1, top, cols(right)], v_s.at[4], v_r.at[4], partner)

    @pl.when(near)
    def _():
        weights(4)

    got(own_p, p_r.at[1])
    got(key_p, p_r.at[2])
    slot[1] = places(own_p[...])
    own_res.wait()
    got(res2.at[1], p_r.at[3])
    for h in range(2):
        acc[h] = res2[:, :, h * PART : (h + 1) * PART].astype(F32)

    @pl.when(near)
    def _():
        pltpu.make_async_copy(wsh_ref, w.at[block(y)], loc.at[3]).wait()

    @pl.when(far)
    def _():
        got(w.at[half(y, 0)], wz_r.at[0])
        got(w.at[half(y, 1)], wz_r.at[8])
        for k in range(1, 4):
            for h in range(2):
                got(w.at[half((y + NY - k) % NY, h)], wz_r.at[8 + 2 * k - 1 + h])
                got(w.at[half((y + k) % NY, h)], wz_r.at[2 * k - 1 + h])
        got(w.at[half((y + 4) % NY, 0)], wz_r.at[7])
        got(w.at[half((y + 4) % NY, 1)], wz_r.at[15])

    def back_tile(q, h):
        for b in range(2):
            acc[h, b] += dot(vg[b, :, cols(q)], w[h * PART : (h + 1) * PART, cols(q)], ((1,), (1,)))

    back_tile(x, 0)
    back_tile(x, 1)
    got(vg.at[1, top, cols(left)], v_r.at[1])
    got(vg.at[1, low, cols(left)], v_r.at[3])
    back_tile(left, 0)
    back_tile(left, 1)

    across = (x + 2) % NX
    got(vg.at[0, top, cols(across)], x_r.at[4])
    send(vg.at[0, top, cols(across)], vg.at[1, top, cols(across)], v_s.at[5], v_r.at[5], partner)
    got(vg.at[0, low, cols(across)], x_r.at[5])
    send(vg.at[0, low, cols(across)], vg.at[1, low, cols(across)], v_s.at[6], v_r.at[6], partner)

    got(vg.at[1, low, cols(right)], v_r.at[2])
    got(vg.at[1, top, cols(right)], v_r.at[4])
    back_tile(right, 0)
    back_tile(right, 1)
    got(vg.at[1, top, cols(across)], v_r.at[5])
    got(vg.at[1, low, cols(across)], v_r.at[6])

    line = lax.broadcasted_iota(jnp.int32, (2 * SLOTS, 1), 0)
    keys = [jnp.broadcast_to((ref[...] + 1).astype(F32), (8, TOK)).astype(BF) for ref in (key_ref, key_p)]

    def pack(d, h):
        to = (y + d) % NY
        wanted = (line // SLOTS) * (NY * SLOTS) + to * SLOTS + line % SLOTS
        for b in range(2):
            pick = (wanted == slot[b]).astype(F32).astype(BF)
            pk[h, d, pl.ds(b * 2 * SLOTS, 2 * SLOTS)] = dot(pick, igb[h, b], ((1,), (0,))).astype(BF)
            if h == 0:
                km[d, :, pl.ds(b * 2 * SLOTS, 2 * SLOTS)] = dot(keys[b], pick, ((1,), (1,)))
        if d > 0:
            if h == 0:
                send(km.at[d], kmr.at[d], m_s.at[d], m_r.at[d], at(y_=to))
            send(pk.at[h, d], kr.at[h, d], k_s.at[8 * h + d], k_r.at[8 * h + d], at(y_=to))

    for h in range(2):
        back_tile(across, h)
        igb[h] = acc[h].astype(BF)
        for d in (*ORDER, 0):
            pack(d, h)

    weight_tile(left)
    weight_tile(right)
    weight_tile(across)

    def rows(r):
        return pl.ds(r * PART, PART)

    def hop(way, s, r, src, dst):
        number = 8 * way + 2 * s + r
        send(src, dst, c_s.at[number], c_r.at[number], up if way == 0 else down)

    def goal(way, s):
        return (z + 4 - s) % NZ if way == 0 else (z + 4 + s) % NZ

    for way in range(2):
        hop(way, 0, way, wp.at[goal(way, 0), rows(way)], cr.at[way, 0, rows(way)])
    for way in range(2):
        hop(way, 1, 1 - way, wp.at[goal(way, 1), rows(1 - way)], cr.at[way, 1, rows(1 - way)])
    for s in range(1, 4):
        for turn in range(2):
            for way in range(2):
                r = 1 - way if turn == 0 else way
                if s == 1 and r != way:
                    continue
                got(cr.at[way, s - 1, rows(r)], c_r.at[8 * way + 2 * (s - 1) + r])
                total = wp[goal(way, s), rows(r)].astype(F32) + cr[way, s - 1, rows(r)].astype(F32)
                if s < 3:
                    cs[way, s - 1, rows(r)] = total.astype(BF)
                    hop(way, s, r, cs.at[way, s - 1, rows(r)], cr.at[way, s, rows(r)])
                else:
                    cfs[way, rows(r)] = total
                    hop(way, s, r, cfs.at[way, rows(r)], cfr.at[way, rows(r)])

    lane = lax.broadcasted_iota(jnp.int32, (1, 4 * SLOTS), 1)
    offset = ((lane // SLOTS) % 2) * KEYS - 1

    def tally(rows_, marks):
        named = marks[0:1, :].astype(jnp.int32)
        number = jnp.where(named > 0, named + offset, -1)
        hit = (lax.broadcasted_iota(jnp.int32, (2 * KEYS, 4 * SLOTS), 0) == number).astype(F32).astype(BF)
        return dot(hit, rows_, ((1,), (0,)))

    def piece(place):
        return block((place % 2) * NH + place // 2)

    def tables(h):
        table[h] = tally(pk[h, 0], km[0])
        for d in ORDER:
            if h == 0:
                got(kmr.at[d], m_r.at[d])
            got(kr.at[h, d], k_r.at[8 * h + d])
            table[h] += tally(kr[h, d], kmr[d])
        tb[h] = table[h].astype(BF)
        for d in ORDER:
            to = (z + d) % NZ
            send(tb.at[h, piece(to)], zr.at[h, d], z_s.at[8 * h + d], z_r.at[8 * h + d], at(z_=to))

    def strip(i, h):
        return pl.ds(pl.multiple_of(i * FEAT + h * PART, PART), PART)

    def finish_keys(h):
        total = table[h, piece(z), :]
        for d in ORDER:
            got(zr.at[h, d], z_r.at[8 * h + d])
            total = total + zr[h, d].astype(F32)
        kb[h] = total.astype(BF)
        here = kout.at[block(zh), strip(c, h)]
        for e in (2, 1, 3):
            send(kb.at[h], here, d_s.at[4 * h + e], d_r.at[4 * h + e], at(z_=((zh + e) % NH) * 2 + zl))
        send(kb.at[h], here, e_s.at[4 * h], e_r.at[4 * h], partner)
        pltpu.make_async_copy(kb.at[h], here, loc.at[4 + h]).start()

    def pass_keys(h):
        for e in (1, 3, 2):
            here = kout.at[block((zh + NH - e) % NH), strip(c, h)]
            got(here, d_r.at[4 * h + e])
            send(here, here, e_s.at[4 * h + e], e_r.at[4 * h + e], partner)

    for r in range(2):
        for way in range(2):
            got(cfr.at[way, rows(r)], c_r.at[8 * way + 6 + r])
        total = wp[z, rows(r)].astype(F32) + cfr[0, rows(r)] + cfr[1, rows(r)]
        ctot[rows(r)] = total
        ws[rows(r)] = total.astype(BF)
    for d in ORDER:
        to = (y + d) % NY
        send(ws.at[block(to)], yr.at[d], b_s.at[d], b_r.at[d], at(y_=to))

    tables(0)
    finish_keys(0)
    pass_keys(0)
    tables(1)

    total = ctot[block(y), :]
    for d in ORDER:
        got(yr.at[d], b_r.at[d])
        total = total + yr[d].astype(F32)
    wf[...] = total

    def heads(i):
        return pl.ds(pl.multiple_of(i * COLS, COLS), COLS)

    for e in (2, 1, 3):
        send(wf, wout.at[:, heads(z)], f_s.at[e], f_r.at[z], at(z_=((zh + e) % NH) * 2 + c))

    @pl.when(far)
    def _():
        send(wf, wout.at[:, heads(z)], f_s.at[0], f_r.at[z], at(z_=zh * 2 + c), False)

    @pl.when(near)
    def _():
        pltpu.make_async_copy(wf, wout.at[:, heads(z)], loc.at[6]).start()
        send(wf, wout.at[:, heads(z)], g_s.at[0], g_r.at[0], partner, False)

    finish_keys(1)

    @pl.when(near)
    def _():
        for d in (1, 7, 2, 6, 3, 5, 4):
            here = wout.at[:, heads((z + d) % NZ)]
            got(here, f_r.at[(z + d) % NZ])
            send(here, here, g_s.at[d], g_r.at[d], partner, False)

    pass_keys(1)

    @pl.when(far)
    def _():
        for d in range(NZ):
            got(wout.at[:, heads((z + d) % NZ)], g_r.at[d])

    for h in range(2):
        for e in range(NH):
            got(kout.at[block((zh + NH - e) % NH), strip(1 - c, h)], e_r.at[4 * h + e])
        got(kb.at[h], loc.at[4 + h])

    for src, sem in ended:
        got(src, sem)

    @pl.when(near)
    def _():
        for number in (0, 1, 2, 3, 4, 5, 6, 8, 9, 10, 11, 12, 13, 15):
            got(wsh_ref.at[first], wy_s.at[number])
        for number in range(16):
            got(wsh_ref.at[first], wz_s.at[number])
        for d in range(NZ):
            got(wf, g_s.at[d])
        got(wf, loc.at[6])

    @pl.when(far)
    def _():
        got(wf, f_s.at[0])


def body(layer_input, value_grad, residual_grad, value_weight, owner, key_row):
    dma = pltpu.SemaphoreType.DMA
    vmem = pl.BlockSpec(memory_space=pltpu.VMEM)
    hbm = pl.BlockSpec(memory_space=pl.ANY)
    scratch = [
        pltpu.VMEM((2, TOK, WIDTH), BF),
        pltpu.VMEM((2, TOK, FEAT), BF),
        pltpu.VMEM((2, TOK, FEAT), BF),
        pltpu.VMEM((1, TOK), jnp.int32),
        pltpu.VMEM((1, TOK), jnp.int32),
        pltpu.VMEM((FEAT, WIDTH), BF),
        pltpu.VMEM((NZ, FEAT, COLS), BF),
        pltpu.VMEM((2, 3, FEAT, COLS), BF),
        pltpu.VMEM((2, 2, FEAT, COLS), BF),
        pltpu.VMEM((2, FEAT, COLS), F32),
        pltpu.VMEM((2, FEAT, COLS), F32),
        pltpu.VMEM((FEAT, COLS), F32),
        pltpu.VMEM((FEAT, COLS), BF),
        pltpu.VMEM((NY, ROWS, COLS), BF),
        pltpu.VMEM((ROWS, COLS), F32),
        pltpu.VMEM((2, 2, TOK, PART), F32),
        pltpu.VMEM((2, 2, TOK, PART), BF),
        pltpu.VMEM((2, NY, 4 * SLOTS, PART), BF),
        pltpu.VMEM((NY, 8, 4 * SLOTS), F32),
        pltpu.VMEM((2, NY, 4 * SLOTS, PART), BF),
        pltpu.VMEM((NY, 8, 4 * SLOTS), F32),
        pltpu.VMEM((2, 2 * KEYS, PART), F32),
        pltpu.VMEM((2, 2 * KEYS, PART), BF),
        pltpu.VMEM((2, NZ, ROWS, PART), BF),
        pltpu.VMEM((2, ROWS, PART), BF),
        dma((7,)),
    ]
    for number in (4, 6, 7, 16, 16, 16, 16, 8, 8, 16, 8, 8):
        scratch += [dma((number,)), dma((number,))]
    scratch += [dma((4,)), dma((8,)), dma((8,)), dma((8,))]
    weight_grad, key_grad = pl.pallas_call(
        kernel,
        out_shape=(
            jax.ShapeDtypeStruct((ROWS, WIDTH), F32),
            jax.ShapeDtypeStruct((KEYS, 2 * FEAT), BF),
        ),
        in_specs=[hbm, hbm, hbm, hbm, vmem, vmem],
        out_specs=(hbm, hbm),
        scratch_shapes=scratch,
        compiler_params=pltpu.CompilerParams(
            collective_id=0, has_side_effects=True, vmem_limit_bytes=60 * 1024 * 1024
        ),
    )(layer_input, value_grad, residual_grad, value_weight, owner.reshape(1, TOK), key_row.reshape(1, TOK))
    return weight_grad, key_grad.astype(F32)


def solution(mesh):
    return jax.shard_map(
        body,
        mesh=mesh,
        in_specs=(
            P(("dp", "fsdp"), "tp"),
            P(("dp", "fsdp"), "tp"),
            P(("dp", "fsdp"), "tp"),
            P(("tp", "fsdp"), None),
            P(("dp", "fsdp"), None),
            P(("dp", "fsdp")),
        ),
        out_specs=(P(("tp", "fsdp"), None), P("fsdp", "tp")),
        check_vma=False,
    )
```

```python
import jax
import jax.numpy as jnp
from jax import lax
from jax.experimental import pallas as pl
from jax.experimental.pallas import tpu as pltpu
from jax.sharding import PartitionSpec as P

MESH = pl.DeviceIdType.MESH
BF, F32 = jnp.bfloat16, jnp.float32
NX, NY, NZ, NH = 4, 8, 8, 4
TOK, FEAT, HEADS, WIDTH = 512, 512, 512, 2048
SLOTS, KEYS, ROWS, COLS = 64, 256, 64, 256
HALF = TOK // 2
PART = FEAT // 2
ORDER = (4, 3, 5, 2, 6, 1, 7)
CHUNKS = ((0, 256), (256, 128), (384, 128))
REST = pl.ds(1, NY - 1)


def dot(a, b, dims):
    return lax.dot_general(a, b, (dims, ((), ())), preferred_element_type=F32)


def kernel(
    li_ref, vgr_ref, res_ref, wsh_ref, own_ref, key_ref,
    wout, kout,
    vg, li2, res2, own_p, key_p, w, wp, cr, cs, cfs, cfr, ctot, ws, yr, wf, acc, igb, pk0, pk1, pk2, km, kr0, kr1, kr2, kmr, table, tb0, tb1, tb2, zr0, zr1, zr2, kb0, kb1, kb2,
    loc, p_s, p_r, x_s, x_r, v_s, v_r, wy_s, wy_r, wz_s, wz_r,
    c_s, c_r, k_s, k_r, m_s, m_r, b_s, b_r, z_s, z_r, d_s, d_r, e_s, e_r, f_s, f_r, g_s, g_r,
):
    dp, fs, x = lax.axis_index("dp"), lax.axis_index("fsdp"), lax.axis_index("tp")
    zh, c, zl, y = dp // 2, dp % 2, fs // NY, fs % NY
    z = zh * 2 + zl
    near = zl == c
    far = zl != c

    def at(x_=x, y_=y, z_=z, c_=c):
        return ((z_ // 2) * 2 + c_, (z_ % 2) * NY + y_, x_)

    partner = at(c_=1 - c)
    right, left = (x + 1) % NX, (x + NX - 1) % NX
    pk, kr, tb = (pk0, pk1, pk2), (kr0, kr1, kr2), (tb0, tb1, tb2)
    zr, kb = (zr0, zr1, zr2), (kb0, kb1, kb2)

    def send(src, dst, ss, rs, to):
        pltpu.make_async_remote_copy(
            src_ref=src, dst_ref=dst, send_sem=ss, recv_sem=rs, device_id=to, device_id_type=MESH
        ).start()

    def got(dst, rs):
        pltpu.make_async_copy(dst, dst, rs).wait()

    def cols(i):
        return pl.ds(pl.multiple_of(i * HEADS, HEADS), HEADS)

    def mine(i):
        return pl.ds(pl.multiple_of(i * FEAT, FEAT), FEAT)

    def half(i, h):
        return pl.ds(pl.multiple_of(i * ROWS + h * 32, 32), 32)

    def block(i):
        return pl.ds(pl.multiple_of(i * ROWS, ROWS), ROWS)

    barrier = pltpu.get_barrier_semaphore()
    peers = [partner, at(x_=right), at(x_=left)]
    peers += [at(y_=(y + d) % NY) for d in range(1, NY)] + [at(z_=(z + d) % NZ) for d in range(1, NZ)]
    for peer in peers:
        pl.semaphore_signal(barrier, inc=1, device_id=peer, device_id_type=MESH)

    own_vg = pltpu.make_async_copy(vgr_ref, vg.at[0, :, cols(x)], loc.at[0])
    own_vg.start()
    own_li = pltpu.make_async_copy(li_ref.at[:, mine(c)], li2.at[0], loc.at[1])
    own_li.start()
    own_res = pltpu.make_async_copy(res_ref.at[:, mine(c)], res2.at[0], loc.at[2])
    own_res.start()

    @pl.when(near)
    def _():
        pltpu.make_async_copy(wsh_ref, w.at[block(y)], loc.at[3]).start()

    pl.semaphore_wait(barrier, len(peers))

    up, down = at(z_=(z + 1) % NZ), at(z_=(z + NZ - 1) % NZ)
    after, before = at(y_=(y + 1) % NY), at(y_=(y + NY - 1) % NY)
    first, second = pl.ds(0, 32), pl.ds(32, 32)

    @pl.when(near)
    def _():
        for h, rows in enumerate((first, second)):
            send(wsh_ref.at[rows], w.at[half(y, h)], wy_s.at[0], wy_r.at[h], after)
            send(wsh_ref.at[rows], w.at[half(y, h)], wy_s.at[0], wy_r.at[8 + h], before)
        send(wsh_ref.at[first], w.at[half(y, 0)], wz_s.at[0], wz_r.at[0], up)
        send(wsh_ref.at[second], w.at[half(y, 1)], wz_s.at[0], wz_r.at[0], down)

    top, low = pl.ds(0, HALF), pl.ds(HALF, HALF)
    send(vgr_ref.at[top], vg.at[0, top, cols(x)], x_s.at[0], x_r.at[0], at(x_=right))
    send(vgr_ref.at[low], vg.at[0, low, cols(x)], x_s.at[0], x_r.at[2], at(x_=left))
    send(vgr_ref.at[low], vg.at[0, low, cols(x)], x_s.at[0], x_r.at[1], at(x_=right))
    send(vgr_ref.at[top], vg.at[0, top, cols(x)], x_s.at[0], x_r.at[3], at(x_=left))
    send(vgr_ref, vg.at[1, :, cols(x)], v_s.at[0], v_r.at[0], partner)
    send(li_ref.at[:, mine(1 - c)], li2.at[1], p_s.at[0], p_r.at[0], partner)
    send(own_ref, own_p, p_s.at[1], p_r.at[1], partner)
    send(key_ref, key_p, p_s.at[2], p_r.at[2], partner)
    send(res_ref.at[:, mine(1 - c)], res2.at[1], p_s.at[0], p_r.at[3], partner)

    def weights(k):
        plus, minus = (y + NY - k) % NY, (y + k) % NY
        for h in range(2):
            for base, shard, onward, side, keeps in ((0, plus, after, down, 0), (8, minus, before, up, 1)):
                if k == 4 and h != keeps:
                    continue
                here = w.at[half(shard, h)]
                got(here, wy_r.at[base + 2 * (k - 1) + h])
                if k < 3 or (k == 3 and h == keeps):
                    send(here, here, wy_s.at[0], wy_r.at[base + 2 * k + h], onward)
                if k < 4:
                    send(here, here, wz_s.at[0], wz_r.at[0], side)
                else:
                    send(here, here, wz_s.at[0], wz_r.at[0], up if base == 0 else down)

    def places(owner):
        hot = (lax.broadcasted_iota(jnp.int32, (16, TOK), 0) == owner).astype(F32)
        order = lax.broadcasted_iota(jnp.int32, (TOK, TOK), 0) <= lax.broadcasted_iota(jnp.int32, (TOK, TOK), 1)
        count = dot(hot.astype(BF), order.astype(F32).astype(BF), ((1,), (0,)))
        rank = jnp.sum(count * hot, axis=0, keepdims=True) - 1.0
        return owner * SLOTS + rank.astype(jnp.int32)

    slot = [places(own_ref[...]), None]

    @pl.when(near)
    def _():
        weights(1)

    got(vg.at[0, top, cols(left)], x_r.at[0])
    send(vg.at[0, top, cols(left)], vg.at[0, top, cols(left)], x_s.at[0], x_r.at[4], at(x_=right))
    send(vg.at[0, top, cols(left)], vg.at[1, top, cols(left)], v_s.at[0], v_r.at[1], partner)
    got(vg.at[0, low, cols(right)], x_r.at[2])
    send(vg.at[0, low, cols(right)], vg.at[0, low, cols(right)], x_s.at[0], x_r.at[5], at(x_=left))
    send(vg.at[0, low, cols(right)], vg.at[1, low, cols(right)], v_s.at[0], v_r.at[2], partner)

    @pl.when(near)
    def _():
        weights(2)

    def weight_tile(q):
        total = None
        for b in range(2):
            part = dot(li2[b], vg[b, :, cols(q)], ((0,), (0,))).astype(BF).astype(F32)
            total = part if total is None else total + part
        wp[2 * q] = total[:, :COLS]
        wp[2 * q + 1] = total[:, COLS:]

    own_vg.wait()
    own_li.wait()
    got(li2.at[1], p_r.at[0])
    got(vg.at[1, :, cols(x)], v_r.at[0])
    weight_tile(x)

    got(own_p, p_r.at[1])
    got(key_p, p_r.at[2])
    slot[1] = places(own_p[...])
    own_res.wait()
    got(res2.at[1], p_r.at[3])
    acc[...] = res2[...].astype(F32)

    got(vg.at[0, low, cols(left)], x_r.at[1])
    send(vg.at[0, low, cols(left)], vg.at[1, low, cols(left)], v_s.at[0], v_r.at[1], partner)
    got(vg.at[0, top, cols(right)], x_r.at[3])
    send(vg.at[0, top, cols(right)], vg.at[1, top, cols(right)], v_s.at[0], v_r.at[2], partner)

    @pl.when(near)
    def _():
        weights(3)

    got(vg.at[1, :, cols(left)], v_r.at[1])
    weight_tile(left)
    got(vg.at[1, :, cols(right)], v_r.at[2])
    weight_tile(right)

    @pl.when(near)
    def _():
        weights(4)

    across = (x + 2) % NX
    got(vg.at[0, top, cols(across)], x_r.at[4])
    send(vg.at[0, top, cols(across)], vg.at[1, top, cols(across)], v_s.at[0], v_r.at[3], partner)
    got(vg.at[0, low, cols(across)], x_r.at[5])
    send(vg.at[0, low, cols(across)], vg.at[1, low, cols(across)], v_s.at[0], v_r.at[3], partner)

    @pl.when(near)
    def _():
        pltpu.make_async_copy(wsh_ref, w.at[block(y)], loc.at[3]).wait()

    @pl.when(far)
    def _():
        got(w, wz_r.at[0])

    def back_tile(q, h=None):
        start, size = (0, FEAT) if h is None else CHUNKS[h]
        for b in range(2):
            acc[b, :, start : start + size] += dot(vg[b, :, cols(q)], w[start : start + size, cols(q)], ((1,), (1,)))

    back_tile(x)
    back_tile(left)
    back_tile(right)
    got(vg.at[1, :, cols(across)], v_r.at[3])

    line = lax.broadcasted_iota(jnp.int32, (2 * SLOTS, 1), 0)
    keys = [jnp.broadcast_to((ref[...] + 1).astype(F32), (8, TOK)).astype(BF) for ref in (key_ref, key_p)]

    def pack(h):
        start, size = CHUNKS[h]
        back_tile(across, h)
        igb[:, :, start : start + size] = acc[:, :, start : start + size].astype(BF)
        for d in (*ORDER, 0):
            to = (y + d) % NY
            wanted = (line // SLOTS) * (NY * SLOTS) + to * SLOTS + line % SLOTS
            for b in range(2):
                pick = (wanted == slot[b]).astype(F32).astype(BF)
                picked = dot(pick, igb[b, :, start : start + size], ((1,), (0,)))
                pk[h][d, pl.ds(b * 2 * SLOTS, 2 * SLOTS)] = picked.astype(BF)
                if h == 0:
                    km[d, :, pl.ds(b * 2 * SLOTS, 2 * SLOTS)] = dot(keys[b], pick, ((1,), (1,)))
            if h < 2 and d > 0:
                ship(h, d)

    def ship(h, d):
        to = at(y_=(y + d) % NY)
        if h == 0:
            send(km.at[d], kmr.at[d], m_s.at[0], m_r.at[0], to)
        send(pk[h].at[d], kr[h].at[d], k_s.at[h], k_r.at[8 * h + d], to)

    def rows(r):
        return pl.ds(r * PART, PART)

    def hop(way, s, r, src, dst):
        number = 8 * way + 2 * s + r
        send(src, dst, c_s.at[0], c_r.at[number], up if way == 0 else down)

    def goal(way, s):
        return (z + 4 - s) % NZ if way == 0 else (z + 4 + s) % NZ

    def start(way, s, r):
        cs[way, s, rows(r)] = wp[goal(way, s), rows(r)].astype(BF)
        hop(way, s, r, cs.at[way, s, rows(r)], cr.at[way, s, rows(r)])

    pack(0)
    weight_tile(across)
    for way in range(2):
        start(way, 0, way)
    for way in range(2):
        start(way, 1, 1 - way)
    pack(1)
    for s in range(1, 4):
        if s == 2:
            pack(2)
        for turn in range(2):
            for way in range(2):
                r = 1 - way if turn == 0 else way
                if s == 1 and r != way:
                    continue
                got(cr.at[way, s - 1, rows(r)], c_r.at[8 * way + 2 * (s - 1) + r])
                total = wp[goal(way, s), rows(r)] + cr[way, s - 1, rows(r)].astype(F32)
                if s < 3:
                    cs[way, s, rows(r)] = total.astype(BF)
                    hop(way, s, r, cs.at[way, s, rows(r)], cr.at[way, s, rows(r)])
                else:
                    cfs[way, rows(r)] = total
                    hop(way, s, r, cfs.at[way, rows(r)], cfr.at[way, rows(r)])

    lane = lax.broadcasted_iota(jnp.int32, (1, 4 * SLOTS), 1)
    offset = ((lane // SLOTS) % 2) * KEYS - 1

    def tally(rows_, marks):
        named = marks[0:1, :].astype(jnp.int32)
        number = jnp.where(named > 0, named + offset, -1)
        hit = (lax.broadcasted_iota(jnp.int32, (2 * KEYS, 4 * SLOTS), 0) == number).astype(F32).astype(BF)
        return dot(hit, rows_, ((1,), (0,)))

    def piece(place):
        return block((place % 2) * NH + place // 2)

    def tables(h):
        start, size = CHUNKS[h]
        here = pl.ds(start, size)
        if h == 0:
            got(kmr.at[REST], m_r.at[0])
        table[:, here] = tally(pk[h][0], km[0])
        for d in ORDER:
            got(kr[h].at[d], k_r.at[8 * h + d])
            table[:, here] += tally(kr[h][d], kmr[d])
        tb[h][...] = table[:, here].astype(BF)
        for d in ORDER:
            to = (z + d) % NZ
            send(tb[h].at[piece(to)], zr[h].at[d], z_s.at[h], z_r.at[h], at(z_=to))

    def strip(i, h):
        start, size = CHUNKS[h]
        return pl.ds(pl.multiple_of(i * FEAT + start, 128), size)

    def finish_keys(h):
        start, size = CHUNKS[h]
        got(zr[h].at[REST], z_r.at[h])
        total = table[piece(z), pl.ds(start, size)]
        for d in ORDER:
            total = total + zr[h][d].astype(F32)
        kb[h][...] = total.astype(BF)
        here = kout.at[block(zh), strip(c, h)]
        for e in (2, 1, 3):
            send(kb[h], here, d_s.at[0], d_r.at[4 * h + e], at(z_=((zh + e) % NH) * 2 + zl))
        send(kb[h], here, e_s.at[0], e_r.at[0], partner)
        pltpu.make_async_copy(kb[h], here, loc.at[4 + h]).start()

    def pass_keys(h):
        for e in (1, 3, 2):
            here = kout.at[block((zh + NH - e) % NH), strip(c, h)]
            got(here, d_r.at[4 * h + e])
            send(here, here, e_s.at[0], e_r.at[0], partner)

    tables(0)

    for r in range(2):
        for way in range(2):
            got(cfr.at[way, rows(r)], c_r.at[8 * way + 6 + r])
        total = wp[z, rows(r)] + cfr[0, rows(r)] + cfr[1, rows(r)]
        ctot[rows(r)] = total
        ws[rows(r)] = total.astype(BF)
    for d in ORDER:
        to = (y + d) % NY
        send(ws.at[block(to)], yr.at[d], b_s.at[0], b_r.at[0], at(y_=to))
    for d in ORDER:
        ship(2, d)

    tables(1)
    finish_keys(0)

    got(yr.at[REST], b_r.at[0])
    total = ctot[block(y), :]
    for d in ORDER:
        total = total + yr[d].astype(F32)
    wf[...] = total

    def heads(i):
        return pl.ds(pl.multiple_of(i * COLS, COLS), COLS)

    for e in (2, 1, 3):
        send(wf, wout.at[:, heads(z)], f_s.at[0], f_r.at[z], at(z_=((zh + e) % NH) * 2 + c))

    @pl.when(far)
    def _():
        send(wf, wout.at[:, heads(z)], f_s.at[0], f_r.at[z], at(z_=zh * 2 + c))

    @pl.when(near)
    def _():
        pltpu.make_async_copy(wf, wout.at[:, heads(z)], loc.at[7]).start()
        send(wf, wout.at[:, heads(z)], g_s.at[0], g_r.at[0], partner)

    finish_keys(1)
    pass_keys(0)
    tables(2)
    pass_keys(1)

    @pl.when(near)
    def _():
        for d in (1, 7, 2, 6, 3, 5, 4):
            here = wout.at[:, heads((z + d) % NZ)]
            got(here, f_r.at[(z + d) % NZ])
            send(here, here, g_s.at[0], g_r.at[0], partner)

    finish_keys(2)
    pass_keys(2)

    @pl.when(far)
    def _():
        got(wout, g_r.at[0])

    got(kout.at[:, mine(1 - c)], e_r.at[0])
    for h in range(3):
        got(kb[h], loc.at[4 + h])

    got(vg.at[0, :, pl.ds(0, 3 * HEADS)], x_s.at[0])
    got(vg.at[0], v_s.at[0])
    got(li2, p_s.at[0])
    got(own_p, p_s.at[1])
    got(key_p, p_s.at[2])
    got(vg.at[:, pl.ds(0, 288)], c_s.at[0])
    for h in range(3):
        got(kr[h].at[REST], k_s.at[h])
        got(zr[h].at[REST], z_s.at[h])
    got(kmr.at[REST], m_s.at[0])
    got(yr.at[REST], b_s.at[0])
    got(w.at[pl.ds(0, 48)], d_s.at[0])
    got(w.at[pl.ds(0, 64)], e_s.at[0])

    @pl.when(near)
    def _():
        got(w.at[pl.ds(0, 448)], wy_s.at[0])
        got(w, wz_s.at[0])
        got(w.at[pl.ds(0, 48)], f_s.at[0])
        got(w.at[pl.ds(0, 128)], g_s.at[0])
        got(wf, loc.at[7])

    @pl.when(far)
    def _():
        got(w.at[pl.ds(0, 64)], f_s.at[0])


def body(layer_input, value_grad, residual_grad, value_weight, owner, key_row):
    dma = pltpu.SemaphoreType.DMA
    vmem = pl.BlockSpec(memory_space=pltpu.VMEM)
    hbm = pl.BlockSpec(memory_space=pl.ANY)
    scratch = [
        pltpu.VMEM((2, TOK, WIDTH), BF),
        pltpu.VMEM((2, TOK, FEAT), BF),
        pltpu.VMEM((2, TOK, FEAT), BF),
        pltpu.VMEM((1, TOK), jnp.int32),
        pltpu.VMEM((1, TOK), jnp.int32),
        pltpu.VMEM((FEAT, WIDTH), BF),
        pltpu.VMEM((NZ, FEAT, COLS), F32),
        pltpu.VMEM((2, 3, FEAT, COLS), BF),
        pltpu.VMEM((2, 3, FEAT, COLS), BF),
        pltpu.VMEM((2, FEAT, COLS), F32),
        pltpu.VMEM((2, FEAT, COLS), F32),
        pltpu.VMEM((FEAT, COLS), F32),
        pltpu.VMEM((FEAT, COLS), BF),
        pltpu.VMEM((NY, ROWS, COLS), BF),
        pltpu.VMEM((ROWS, COLS), F32),
        pltpu.VMEM((2, TOK, FEAT), F32),
        pltpu.VMEM((2, TOK, FEAT), BF),
    ]
    widths = [size for _, size in CHUNKS]
    scratch += [pltpu.VMEM((NY, 4 * SLOTS, size), BF) for size in widths]
    scratch += [pltpu.VMEM((NY, 8, 4 * SLOTS), F32)]
    scratch += [pltpu.VMEM((NY, 4 * SLOTS, size), BF) for size in widths]
    scratch += [pltpu.VMEM((NY, 8, 4 * SLOTS), F32), pltpu.VMEM((2 * KEYS, FEAT), F32)]
    scratch += [pltpu.VMEM((2 * KEYS, size), BF) for size in widths]
    scratch += [pltpu.VMEM((NZ, ROWS, size), BF) for size in widths]
    scratch += [pltpu.VMEM((ROWS, size), BF) for size in widths]
    scratch += [dma((8,))]
    for sent, received in ((3, 4), (1, 6), (1, 4), (1, 16), (1, 1), (1, 16), (3, 24), (1, 1), (1, 1), (3, 3), (1, 12), (1, 1)):
        scratch += [dma((sent,)), dma((received,))]
    scratch += [dma((1,)), dma((8,)), dma((1,)), dma((1,))]
    weight_grad, key_grad = pl.pallas_call(
        kernel,
        out_shape=(
            pltpu.VMEM((ROWS, WIDTH), F32),
            pltpu.VMEM((KEYS, 2 * FEAT), BF),
        ),
        in_specs=[hbm, hbm, hbm, hbm, vmem, vmem],
        out_specs=(vmem, vmem),
        scratch_shapes=scratch,
        compiler_params=pltpu.CompilerParams(
            collective_id=0, has_side_effects=True, vmem_limit_bytes=60 * 1024 * 1024
        ),
    )(layer_input, value_grad, residual_grad, value_weight, owner.reshape(1, TOK), key_row.reshape(1, TOK))
    return weight_grad, key_grad.astype(F32)


def solution(mesh):
    return jax.shard_map(
        body,
        mesh=mesh,
        in_specs=(
            P(("dp", "fsdp"), "tp"),
            P(("dp", "fsdp"), "tp"),
            P(("dp", "fsdp"), "tp"),
            P(("tp", "fsdp"), None),
            P(("dp", "fsdp"), None),
            P(("dp", "fsdp")),
        ),
        out_specs=(P(("tp", "fsdp"), None), P("fsdp", "tp")),
        check_vma=False,
    )
```

```python
import jax
import jax.numpy as jnp
from jax import lax
from jax.experimental import pallas as pl
from jax.experimental.pallas import tpu as pltpu
from jax.sharding import PartitionSpec as P

MESH = pl.DeviceIdType.MESH
BF, F32 = jnp.bfloat16, jnp.float32
NX, NY, NZ, NH = 4, 8, 8, 4
TOK, FEAT, HEADS, WIDTH = 512, 512, 512, 2048
SLOTS, KEYS, ROWS, COLS = 64, 256, 64, 256
HALF = TOK // 2
PART = FEAT // 2
ORDER = (4, 3, 5, 2, 6, 1, 7)
CHUNKS = ((0, 256), (256, 128), (384, 128))
REST = pl.ds(1, NY - 1)


def dot(a, b, dims):
    return lax.dot_general(a, b, (dims, ((), ())), preferred_element_type=F32)


def kernel(
    li_ref, vgr_ref, res_ref, wsh_ref, own_ref, key_ref,
    wout, kout,
    vg, li2, res2, own_p, key_p, w, wp, cr, cs, cfs, cfr, ctot, ws, yr, wf, acc, igb, pk0, pk1, pk2, km, kr0, kr1, kr2, kmr, table, tb0, tb1, tb2, zr0, zr1, zr2, kb0, kb1, kb2, gt0, gt1, gt2, gr0, gr1, gr2,
    loc, p_s, p_r, x_s, x_r, v_s, v_r, wy_s, wy_r, wz_s, wz_r,
    c_s, c_r, k_s, k_r, m_s, m_r, b_s, b_r, z_s, z_r, d_s, d_r, e_s, e_r, f_s, f_r, g_s, g_r, n_s, n_r,
):
    dp, fs, x = lax.axis_index("dp"), lax.axis_index("fsdp"), lax.axis_index("tp")
    zh, c, zl, y = dp // 2, dp % 2, fs // NY, fs % NY
    z = zh * 2 + zl
    near = zl == c
    far = zl != c

    def at(x_=x, y_=y, z_=z, c_=c):
        return ((z_ // 2) * 2 + c_, (z_ % 2) * NY + y_, x_)

    partner = at(c_=1 - c)
    right, left = (x + 1) % NX, (x + NX - 1) % NX
    pk, kr, tb = (pk0, pk1, pk2), (kr0, kr1, kr2), (tb0, tb1, tb2)
    zr, kb, gt, gr = (zr0, zr1, zr2), (kb0, kb1, kb2), (gt0, gt1, gt2), (gr0, gr1, gr2)

    def send(src, dst, ss, rs, to):
        pltpu.make_async_remote_copy(
            src_ref=src, dst_ref=dst, send_sem=ss, recv_sem=rs, device_id=to, device_id_type=MESH
        ).start()

    def got(dst, rs):
        pltpu.make_async_copy(dst, dst, rs).wait()

    def cols(i):
        return pl.ds(pl.multiple_of(i * HEADS, HEADS), HEADS)

    def mine(i):
        return pl.ds(pl.multiple_of(i * FEAT, FEAT), FEAT)

    def half(i, h):
        return pl.ds(pl.multiple_of(i * ROWS + h * 32, 32), 32)

    def block(i):
        return pl.ds(pl.multiple_of(i * ROWS, ROWS), ROWS)

    barrier = pltpu.get_barrier_semaphore()
    peers = [partner, at(x_=right), at(x_=left)]
    peers += [at(y_=(y + d) % NY) for d in range(1, NY)] + [at(z_=(z + d) % NZ) for d in range(1, NZ)]
    for peer in peers:
        pl.semaphore_signal(barrier, inc=1, device_id=peer, device_id_type=MESH)

    own_vg = pltpu.make_async_copy(vgr_ref, vg.at[0, :, cols(x)], loc.at[0])
    own_vg.start()
    own_li = pltpu.make_async_copy(li_ref.at[:, mine(c)], li2.at[0], loc.at[1])
    own_li.start()
    own_res = pltpu.make_async_copy(res_ref.at[:, mine(c)], res2.at[0], loc.at[2])
    own_res.start()

    @pl.when(near)
    def _():
        pltpu.make_async_copy(wsh_ref, w.at[block(y)], loc.at[3]).start()

    pl.semaphore_wait(barrier, len(peers))

    up, down = at(z_=(z + 1) % NZ), at(z_=(z + NZ - 1) % NZ)
    after, before = at(y_=(y + 1) % NY), at(y_=(y + NY - 1) % NY)
    first, second = pl.ds(0, 32), pl.ds(32, 32)

    @pl.when(near)
    def _():
        for h, rows in enumerate((first, second)):
            send(wsh_ref.at[rows], w.at[half(y, h)], wy_s.at[0], wy_r.at[h], after)
            send(wsh_ref.at[rows], w.at[half(y, h)], wy_s.at[0], wy_r.at[8 + h], before)
        send(wsh_ref.at[first], w.at[half(y, 0)], wz_s.at[0], wz_r.at[0], up)
        send(wsh_ref.at[second], w.at[half(y, 1)], wz_s.at[0], wz_r.at[0], down)

    top, low = pl.ds(0, HALF), pl.ds(HALF, HALF)
    send(vgr_ref.at[top], vg.at[0, top, cols(x)], x_s.at[0], x_r.at[0], at(x_=right))
    send(vgr_ref.at[low], vg.at[0, low, cols(x)], x_s.at[0], x_r.at[2], at(x_=left))
    send(vgr_ref.at[low], vg.at[0, low, cols(x)], x_s.at[0], x_r.at[1], at(x_=right))
    send(vgr_ref.at[top], vg.at[0, top, cols(x)], x_s.at[0], x_r.at[3], at(x_=left))
    send(own_ref, own_p, p_s.at[1], p_r.at[1], partner)
    send(key_ref, key_p, p_s.at[2], p_r.at[2], partner)

    def weights(k):
        plus, minus = (y + NY - k) % NY, (y + k) % NY
        for h in range(2):
            for base, shard, onward, side, keeps in ((0, plus, after, down, 0), (8, minus, before, up, 1)):
                if k == 4 and h != keeps:
                    continue
                here = w.at[half(shard, h)]
                got(here, wy_r.at[base + 2 * (k - 1) + h])
                if k < 3 or (k == 3 and h == keeps):
                    send(here, here, wy_s.at[0], wy_r.at[base + 2 * k + h], onward)
                if k < 4:
                    send(here, here, wz_s.at[0], wz_r.at[0], side)
                else:
                    send(here, here, wz_s.at[0], wz_r.at[0], up if base == 0 else down)

    def places(owner):
        hot = (lax.broadcasted_iota(jnp.int32, (16, TOK), 0) == owner).astype(F32)
        order = lax.broadcasted_iota(jnp.int32, (TOK, TOK), 0) <= lax.broadcasted_iota(jnp.int32, (TOK, TOK), 1)
        count = dot(hot.astype(BF), order.astype(F32).astype(BF), ((1,), (0,)))
        rank = jnp.sum(count * hot, axis=0, keepdims=True) - 1.0
        return owner * SLOTS + rank.astype(jnp.int32)

    slot = [places(own_ref[...]), None]

    @pl.when(near)
    def _():
        weights(1)

    send(vgr_ref, vg.at[1, :, cols(x)], v_s.at[0], v_r.at[0], partner)
    send(li_ref.at[:, mine(1 - c)], li2.at[1], p_s.at[0], p_r.at[0], partner)

    got(vg.at[0, top, cols(left)], x_r.at[0])
    send(vg.at[0, top, cols(left)], vg.at[0, top, cols(left)], x_s.at[0], x_r.at[4], at(x_=right))
    send(vg.at[0, top, cols(left)], vg.at[1, top, cols(left)], v_s.at[0], v_r.at[1], partner)
    got(vg.at[0, low, cols(right)], x_r.at[2])
    send(vg.at[0, low, cols(right)], vg.at[0, low, cols(right)], x_s.at[0], x_r.at[5], at(x_=left))
    send(vg.at[0, low, cols(right)], vg.at[1, low, cols(right)], v_s.at[0], v_r.at[2], partner)

    @pl.when(near)
    def _():
        weights(2)

    def weight_tile(q):
        total = None
        for b in range(2):
            part = dot(li2[b], vg[b, :, cols(q)], ((0,), (0,))).astype(BF).astype(F32)
            total = part if total is None else total + part
        wp[2 * q] = total[:, :COLS]
        wp[2 * q + 1] = total[:, COLS:]

    send(res_ref.at[:, mine(1 - c)], res2.at[1], p_s.at[0], p_r.at[3], partner)

    own_vg.wait()
    own_li.wait()
    got(li2.at[1], p_r.at[0])
    got(vg.at[1, :, cols(x)], v_r.at[0])
    weight_tile(x)

    got(own_p, p_r.at[1])
    got(key_p, p_r.at[2])
    slot[1] = places(own_p[...])
    @pl.when(near)
    def _():
        weights(3)

    got(vg.at[0, low, cols(left)], x_r.at[1])
    send(vg.at[0, low, cols(left)], vg.at[1, low, cols(left)], v_s.at[0], v_r.at[1], partner)
    got(vg.at[0, top, cols(right)], x_r.at[3])
    send(vg.at[0, top, cols(right)], vg.at[1, top, cols(right)], v_s.at[0], v_r.at[2], partner)

    @pl.when(near)
    def _():
        weights(4)

    across = (x + 2) % NX
    got(vg.at[0, top, cols(across)], x_r.at[4])
    send(vg.at[0, top, cols(across)], vg.at[1, top, cols(across)], v_s.at[0], v_r.at[3], partner)
    got(vg.at[0, low, cols(across)], x_r.at[5])
    send(vg.at[0, low, cols(across)], vg.at[1, low, cols(across)], v_s.at[0], v_r.at[3], partner)

    own_res.wait()
    got(res2.at[1], p_r.at[3])
    acc[...] = res2[...].astype(F32)

    @pl.when(near)
    def _():
        pltpu.make_async_copy(wsh_ref, w.at[block(y)], loc.at[3]).wait()

    @pl.when(far)
    def _():
        got(w, wz_r.at[0])

    def back_tile(q, h=None):
        start, size = (0, FEAT) if h is None else CHUNKS[h]
        for b in range(2):
            acc[b, :, start : start + size] += dot(vg[b, :, cols(q)], w[start : start + size, cols(q)], ((1,), (1,)))

    back_tile(x)
    got(vg.at[1, :, cols(left)], v_r.at[1])
    back_tile(left)
    got(vg.at[1, :, cols(right)], v_r.at[2])
    back_tile(right)
    got(vg.at[1, :, cols(across)], v_r.at[3])

    line = lax.broadcasted_iota(jnp.int32, (2 * SLOTS, 1), 0)
    keys = [jnp.broadcast_to((ref[...] + 1).astype(F32), (8, TOK)).astype(BF) for ref in (key_ref, key_p)]

    def pack(h):
        start, size = CHUNKS[h]
        back_tile(across, h)
        igb[:, :, start : start + size] = acc[:, :, start : start + size].astype(BF)
        for d in (*ORDER, 0):
            to = (y + d) % NY
            wanted = (line // SLOTS) * (NY * SLOTS) + to * SLOTS + line % SLOTS
            for b in range(2):
                pick = (wanted == slot[b]).astype(F32).astype(BF)
                picked = dot(pick, igb[b, :, start : start + size], ((1,), (0,)))
                pk[h][d, pl.ds(b * 2 * SLOTS, 2 * SLOTS)] = picked.astype(BF)
                if h == 0:
                    km[d, :, pl.ds(b * 2 * SLOTS, 2 * SLOTS)] = dot(keys[b], pick, ((1,), (1,)))
            if h < 2 and 2 <= d <= 6:
                ship(h, d)

    parts = (pl.ds(0, 2 * SLOTS), pl.ds(2 * SLOTS, 2 * SLOTS))

    def ship(h, d):
        for way in range(2):
            if (d, way) in ((2, 1), (3, 1), (5, 0), (6, 0)):
                continue
            place = d - 1 if way == 0 else d + 1
            to = at(y_=(y + place) % NY)
            if h == 0:
                send(km.at[d], kmr.at[place], m_s.at[0], m_r.at[0], to)
            src, dst = pk[h].at[d], kr[h].at[place]
            if d == 4:
                src, dst = pk[h].at[d, parts[way]], kr[h].at[place, parts[way]]
            send(src, dst, k_s.at[h], k_r.at[8 * h + place], to)

    def rows(r):
        return pl.ds(r * PART, PART)

    def hop(way, s, r, src, dst):
        number = 8 * way + 2 * s + r
        send(src, dst, c_s.at[0], c_r.at[number], up if way == 0 else down)

    def goal(way, s):
        return (z + 4 - s) % NZ if way == 0 else (z + 4 + s) % NZ

    def start(way, s, r):
        cs[way, s, rows(r)] = wp[goal(way, s), rows(r)].astype(BF)
        hop(way, s, r, cs.at[way, s, rows(r)], cr.at[way, s, rows(r)])

    def tally(rows_, marks):
        slots = rows_.shape[0]
        lane = lax.broadcasted_iota(jnp.int32, (1, slots), 1)
        named = marks[0:1, :].astype(jnp.int32)
        number = jnp.where(named > 0, named + ((lane // SLOTS) % 2) * KEYS - 1, -1)
        hit = (lax.broadcasted_iota(jnp.int32, (2 * KEYS, slots), 0) == number).astype(F32).astype(BF)
        return dot(hit, rows_, ((1,), (0,)))

    def gate(h):
        if h == 0:
            got(kmr.at[pl.ds(0, 6)], m_r.at[0])
        for way in range(2):
            own, places_ = ((1, (1, 2, 3)), (7, (7, 6, 5)))[way]
            total = tally(pk[h][own], km[own])
            for place in places_:
                if place in (3, 5):
                    got(kr[h].at[place, parts[way]], k_r.at[8 * h + place])
                    total = total + tally(kr[h][place, parts[way]], kmr[place, :, parts[way]])
                else:
                    got(kr[h].at[place], k_r.at[8 * h + place])
                    total = total + tally(kr[h][place], kmr[place])
            gt[h][way] = total.astype(BF)
            to = after if way == 0 else before
            send(gt[h].at[way], gr[h].at[way], n_s.at[h], n_r.at[2 * h + way], to)

    pack(0)
    weight_tile(left)
    weight_tile(right)
    weight_tile(across)
    for way in range(2):
        start(way, 0, way)
    for way in range(2):
        start(way, 1, 1 - way)
    pack(1)
    for s in range(1, 4):
        if s == 2:
            pack(2)
        if s == 3:
            gate(0)
            for d in ORDER[:5]:
                ship(2, d)
        for turn in range(2):
            for way in range(2):
                r = 1 - way if turn == 0 else way
                if s == 1 and r != way:
                    continue
                got(cr.at[way, s - 1, rows(r)], c_r.at[8 * way + 2 * (s - 1) + r])
                total = wp[goal(way, s), rows(r)] + cr[way, s - 1, rows(r)].astype(F32)
                if s < 3:
                    cs[way, s, rows(r)] = total.astype(BF)
                    hop(way, s, r, cs.at[way, s, rows(r)], cr.at[way, s, rows(r)])
                else:
                    cfs[way, rows(r)] = total
                    hop(way, s, r, cfs.at[way, rows(r)], cfr.at[way, rows(r)])

    def piece(place):
        return block((place % 2) * NH + place // 2)

    def tables(h):
        start, size = CHUNKS[h]
        here = pl.ds(start, size)
        table[:, here] = tally(pk[h][0], km[0])
        for way in range(2):
            got(gr[h].at[way], n_r.at[2 * h + way])
            table[:, here] += gr[h][way].astype(F32)
        tb[h][...] = table[:, here].astype(BF)
        for d in ORDER:
            to = (z + d) % NZ
            send(tb[h].at[piece(to)], zr[h].at[d], z_s.at[h], z_r.at[h], at(z_=to))

    def strip(i, h):
        start, size = CHUNKS[h]
        return pl.ds(pl.multiple_of(i * FEAT + start, 128), size)

    def finish_keys(h):
        start, size = CHUNKS[h]
        got(zr[h].at[REST], z_r.at[h])
        total = table[piece(z), pl.ds(start, size)]
        for d in ORDER:
            total = total + zr[h][d].astype(F32)
        kb[h][...] = total.astype(BF)
        here = kout.at[block(zh), strip(c, h)]
        for e in (2, 1, 3):
            send(kb[h], here, d_s.at[0], d_r.at[4 * h + e], at(z_=((zh + e) % NH) * 2 + zl))
        send(kb[h], here, e_s.at[0], e_r.at[0], partner)
        pltpu.make_async_copy(kb[h], here, loc.at[4 + h]).start()

    def pass_keys(h):
        for e in (1, 3, 2):
            here = kout.at[block((zh + NH - e) % NH), strip(c, h)]
            got(here, d_r.at[4 * h + e])
            send(here, here, e_s.at[0], e_r.at[0], partner)

    gate(1)
    tables(0)

    for r in range(2):
        for way in range(2):
            got(cfr.at[way, rows(r)], c_r.at[8 * way + 6 + r])
        total = wp[z, rows(r)] + cfr[0, rows(r)] + cfr[1, rows(r)]
        ctot[rows(r)] = total
        ws[rows(r)] = total.astype(BF)
    gate(2)
    for d in ORDER:
        to = (y + d) % NY
        send(ws.at[block(to)], yr.at[d], b_s.at[0], b_r.at[0], at(y_=to))

    finish_keys(0)
    tables(1)
    tables(2)
    finish_keys(1)
    pass_keys(0)
    finish_keys(2)

    got(yr.at[REST], b_r.at[0])
    total = ctot[block(y), :]
    for d in ORDER:
        total = total + yr[d].astype(F32)
    wf[...] = total

    def heads(i):
        return pl.ds(pl.multiple_of(i * COLS, COLS), COLS)

    for e in (2, 1, 3):
        send(wf, wout.at[:, heads(z)], f_s.at[0], f_r.at[z], at(z_=((zh + e) % NH) * 2 + c))

    @pl.when(far)
    def _():
        send(wf, wout.at[:, heads(z)], f_s.at[0], f_r.at[z], at(z_=zh * 2 + c))

    @pl.when(near)
    def _():
        pltpu.make_async_copy(wf, wout.at[:, heads(z)], loc.at[7]).start()
        send(wf, wout.at[:, heads(z)], g_s.at[0], g_r.at[0], partner)

    pass_keys(1)
    pass_keys(2)

    @pl.when(near)
    def _():
        for d in (1, 7, 2, 6, 3, 5, 4):
            here = wout.at[:, heads((z + d) % NZ)]
            got(here, f_r.at[(z + d) % NZ])
            send(here, here, g_s.at[0], g_r.at[0], partner)

    @pl.when(far)
    def _():
        got(wout, g_r.at[0])

    got(kout.at[:, mine(1 - c)], e_r.at[0])
    for h in range(3):
        got(kb[h], loc.at[4 + h])

    got(vg.at[0, :, pl.ds(0, 3 * HEADS)], x_s.at[0])
    got(vg.at[0], v_s.at[0])
    got(li2, p_s.at[0])
    got(own_p, p_s.at[1])
    got(key_p, p_s.at[2])
    got(vg.at[:, pl.ds(0, 288)], c_s.at[0])
    for h in range(3):
        got(kr[h].at[pl.ds(0, 5)], k_s.at[h])
        got(gr[h], n_s.at[h])
        got(zr[h].at[REST], z_s.at[h])
    got(kmr.at[pl.ds(0, 6)], m_s.at[0])
    got(yr.at[REST], b_s.at[0])
    got(w.at[pl.ds(0, 48)], d_s.at[0])
    got(w.at[pl.ds(0, 64)], e_s.at[0])

    @pl.when(near)
    def _():
        got(w.at[pl.ds(0, 448)], wy_s.at[0])
        got(w, wz_s.at[0])
        got(w.at[pl.ds(0, 48)], f_s.at[0])
        got(w.at[pl.ds(0, 128)], g_s.at[0])
        got(wf, loc.at[7])

    @pl.when(far)
    def _():
        got(w.at[pl.ds(0, 64)], f_s.at[0])


def body(layer_input, value_grad, residual_grad, value_weight, owner, key_row):
    dma = pltpu.SemaphoreType.DMA
    vmem = pl.BlockSpec(memory_space=pltpu.VMEM)
    hbm = pl.BlockSpec(memory_space=pl.ANY)
    scratch = [
        pltpu.VMEM((2, TOK, WIDTH), BF),
        pltpu.VMEM((2, TOK, FEAT), BF),
        pltpu.VMEM((2, TOK, FEAT), BF),
        pltpu.VMEM((1, TOK), jnp.int32),
        pltpu.VMEM((1, TOK), jnp.int32),
        pltpu.VMEM((FEAT, WIDTH), BF),
        pltpu.VMEM((NZ, FEAT, COLS), F32),
        pltpu.VMEM((2, 3, FEAT, COLS), BF),
        pltpu.VMEM((2, 3, FEAT, COLS), BF),
        pltpu.VMEM((2, FEAT, COLS), F32),
        pltpu.VMEM((2, FEAT, COLS), F32),
        pltpu.VMEM((FEAT, COLS), F32),
        pltpu.VMEM((FEAT, COLS), BF),
        pltpu.VMEM((NY, ROWS, COLS), BF),
        pltpu.VMEM((ROWS, COLS), F32),
        pltpu.VMEM((2, TOK, FEAT), F32),
        pltpu.VMEM((2, TOK, FEAT), BF),
    ]
    widths = [size for _, size in CHUNKS]
    scratch += [pltpu.VMEM((NY, 4 * SLOTS, size), BF) for size in widths]
    scratch += [pltpu.VMEM((NY, 8, 4 * SLOTS), F32)]
    scratch += [pltpu.VMEM((NY, 4 * SLOTS, size), BF) for size in widths]
    scratch += [pltpu.VMEM((NY, 8, 4 * SLOTS), F32), pltpu.VMEM((2 * KEYS, FEAT), F32)]
    scratch += [pltpu.VMEM((2 * KEYS, size), BF) for size in widths]
    scratch += [pltpu.VMEM((NZ, ROWS, size), BF) for size in widths]
    scratch += [pltpu.VMEM((ROWS, size), BF) for size in widths]
    scratch += [pltpu.VMEM((2, 2 * KEYS, size), BF) for size in (*widths, *widths)]
    scratch += [dma((8,))]
    for sent, received in ((3, 4), (1, 6), (1, 4), (1, 16), (1, 1), (1, 16), (3, 24), (1, 1), (1, 1), (3, 3), (1, 12), (1, 1)):
        scratch += [dma((sent,)), dma((received,))]
    scratch += [dma((1,)), dma((8,)), dma((1,)), dma((1,)), dma((3,)), dma((6,))]
    weight_grad, key_grad = pl.pallas_call(
        kernel,
        out_shape=(
            pltpu.VMEM((ROWS, WIDTH), F32),
            pltpu.VMEM((KEYS, 2 * FEAT), BF),
        ),
        in_specs=[hbm, hbm, hbm, hbm, vmem, vmem],
        out_specs=(vmem, vmem),
        scratch_shapes=scratch,
        compiler_params=pltpu.CompilerParams(
            collective_id=0, has_side_effects=True, vmem_limit_bytes=60 * 1024 * 1024
        ),
    )(layer_input, value_grad, residual_grad, value_weight, owner.reshape(1, TOK), key_row.reshape(1, TOK))
    return weight_grad, key_grad.astype(F32)


def solution(mesh):
    return jax.shard_map(
        body,
        mesh=mesh,
        in_specs=(
            P(("dp", "fsdp"), "tp"),
            P(("dp", "fsdp"), "tp"),
            P(("dp", "fsdp"), "tp"),
            P(("tp", "fsdp"), None),
            P(("dp", "fsdp"), None),
            P(("dp", "fsdp")),
        ),
        out_specs=(P(("tp", "fsdp"), None), P("fsdp", "tp")),
        check_vma=False,
    )
```

```python
import jax
import jax.numpy as jnp
from jax import lax
from jax.experimental import pallas as pl
from jax.experimental.pallas import tpu as pltpu
from jax.sharding import PartitionSpec as P

MESH = pl.DeviceIdType.MESH
BF, F32 = jnp.bfloat16, jnp.float32
NX, NY, NZ, NH = 4, 8, 8, 4
TOK, FEAT, HEADS, WIDTH = 512, 512, 512, 2048
SLOTS, KEYS, ROWS, COLS = 64, 256, 64, 256
HALF = TOK // 2
PART = FEAT // 2
ORDER = (4, 3, 5, 2, 6, 1, 7)
CHUNKS = ((0, 256), (256, 128), (384, 128))
REST = pl.ds(1, NY - 1)


def dot(a, b, dims):
    return lax.dot_general(a, b, (dims, ((), ())), preferred_element_type=F32)


def kernel(
    li_ref, vgr_ref, res_ref, wsh_ref, own_ref, key_ref,
    wout, kout,
    vg, li2, res2, own_p, key_p, w, wp, cr, cs, cfs, cfr, ctot, ws, yr, wf, acc, igb, pk0, pk1, pk2, km, kr0, kr1, kr2, kmr, table, tb0, tb1, tb2, zr0, zr1, zr2, kb0, kb1, kb2, gt0, gt1, gt2, gr0, gr1, gr2,
    loc, p_s, p_r, x_s, x_r, v_s, v_r, wy_s, wy_r, wz_s, wz_r,
    c_s, c_r, k_s, k_r, m_s, m_r, b_s, b_r, z_s, z_r, d_s, d_r, e_s, e_r, f_s, f_r, g_s, g_r, n_s, n_r,
):
    dp, fs, x = lax.axis_index("dp"), lax.axis_index("fsdp"), lax.axis_index("tp")
    zh, c, zl, y = dp // 2, dp % 2, fs // NY, fs % NY
    z = zh * 2 + zl
    near = zl == c
    far = zl != c

    def at(x_=x, y_=y, z_=z, c_=c):
        return ((z_ // 2) * 2 + c_, (z_ % 2) * NY + y_, x_)

    partner = at(c_=1 - c)
    right, left = (x + 1) % NX, (x + NX - 1) % NX
    pk, kr, tb = (pk0, pk1, pk2), (kr0, kr1, kr2), (tb0, tb1, tb2)
    zr, kb, gt, gr = (zr0, zr1, zr2), (kb0, kb1, kb2), (gt0, gt1, gt2), (gr0, gr1, gr2)

    def send(src, dst, ss, rs, to):
        pltpu.make_async_remote_copy(
            src_ref=src, dst_ref=dst, send_sem=ss, recv_sem=rs, device_id=to, device_id_type=MESH
        ).start()

    def got(dst, rs):
        pltpu.make_async_copy(dst, dst, rs).wait()

    def cols(i):
        return pl.ds(pl.multiple_of(i * HEADS, HEADS), HEADS)

    def mine(i):
        return pl.ds(pl.multiple_of(i * FEAT, FEAT), FEAT)

    def half(i, h):
        return pl.ds(pl.multiple_of(i * ROWS + h * 32, 32), 32)

    def block(i):
        return pl.ds(pl.multiple_of(i * ROWS, ROWS), ROWS)

    barrier = pltpu.get_barrier_semaphore()
    peers = [partner, at(x_=right), at(x_=left)]
    peers += [at(y_=(y + d) % NY) for d in range(1, NY)] + [at(z_=(z + d) % NZ) for d in range(1, NZ)]
    for peer in peers:
        pl.semaphore_signal(barrier, inc=1, device_id=peer, device_id_type=MESH)

    own_vg = pltpu.make_async_copy(vgr_ref, vg.at[0, :, cols(x)], loc.at[0])
    own_vg.start()
    own_li = pltpu.make_async_copy(li_ref.at[:, mine(c)], li2.at[0], loc.at[1])
    own_li.start()
    own_res = pltpu.make_async_copy(res_ref.at[:, mine(c)], res2.at[0], loc.at[2])
    own_res.start()

    @pl.when(near)
    def _():
        pltpu.make_async_copy(wsh_ref, w.at[block(y)], loc.at[3]).start()

    pl.semaphore_wait(barrier, len(peers))

    up, down = at(z_=(z + 1) % NZ), at(z_=(z + NZ - 1) % NZ)
    after, before = at(y_=(y + 1) % NY), at(y_=(y + NY - 1) % NY)
    first, second = pl.ds(0, 32), pl.ds(32, 32)

    @pl.when(near)
    def _():
        for h, rows in enumerate((first, second)):
            send(wsh_ref.at[rows], w.at[half(y, h)], wy_s.at[0], wy_r.at[h], after)
            send(wsh_ref.at[rows], w.at[half(y, h)], wy_s.at[0], wy_r.at[8 + h], before)
        send(wsh_ref.at[first], w.at[half(y, 0)], wz_s.at[0], wz_r.at[0], up)
        send(wsh_ref.at[second], w.at[half(y, 1)], wz_s.at[0], wz_r.at[0], down)

    top, low = pl.ds(0, HALF), pl.ds(HALF, HALF)
    send(vgr_ref.at[top], vg.at[0, top, cols(x)], x_s.at[0], x_r.at[0], at(x_=right))
    send(vgr_ref.at[low], vg.at[0, low, cols(x)], x_s.at[0], x_r.at[2], at(x_=left))
    send(vgr_ref.at[low], vg.at[0, low, cols(x)], x_s.at[0], x_r.at[1], at(x_=right))
    send(vgr_ref.at[top], vg.at[0, top, cols(x)], x_s.at[0], x_r.at[3], at(x_=left))
    send(own_ref, own_p, p_s.at[1], p_r.at[1], partner)
    send(key_ref, key_p, p_s.at[2], p_r.at[2], partner)

    def weights(k):
        plus, minus = (y + NY - k) % NY, (y + k) % NY
        for h in range(2):
            for base, shard, onward, side, keeps in ((0, plus, after, down, 0), (8, minus, before, up, 1)):
                if k == 4 and h != keeps:
                    continue
                here = w.at[half(shard, h)]
                got(here, wy_r.at[base + 2 * (k - 1) + h])
                if k < 3 or (k == 3 and h == keeps):
                    send(here, here, wy_s.at[0], wy_r.at[base + 2 * k + h], onward)
                if k < 4:
                    send(here, here, wz_s.at[0], wz_r.at[0], side)
                else:
                    send(here, here, wz_s.at[0], wz_r.at[0], up if base == 0 else down)

    def places(owner):
        hot = (lax.broadcasted_iota(jnp.int32, (16, TOK), 0) == owner).astype(F32)
        order = lax.broadcasted_iota(jnp.int32, (TOK, TOK), 0) <= lax.broadcasted_iota(jnp.int32, (TOK, TOK), 1)
        count = dot(hot.astype(BF), order.astype(F32).astype(BF), ((1,), (0,)))
        rank = jnp.sum(count * hot, axis=0, keepdims=True) - 1.0
        return owner * SLOTS + rank.astype(jnp.int32)

    slot = [places(own_ref[...]), None]

    @pl.when(near)
    def _():
        weights(1)

    send(vgr_ref, vg.at[1, :, cols(x)], v_s.at[0], v_r.at[0], partner)
    send(li_ref.at[:, mine(1 - c)], li2.at[1], p_s.at[0], p_r.at[0], partner)

    got(vg.at[0, top, cols(left)], x_r.at[0])
    send(vg.at[0, top, cols(left)], vg.at[0, top, cols(left)], x_s.at[0], x_r.at[4], at(x_=right))
    send(vg.at[0, top, cols(left)], vg.at[1, top, cols(left)], v_s.at[0], v_r.at[1], partner)
    got(vg.at[0, low, cols(right)], x_r.at[2])
    send(vg.at[0, low, cols(right)], vg.at[0, low, cols(right)], x_s.at[0], x_r.at[5], at(x_=left))
    send(vg.at[0, low, cols(right)], vg.at[1, low, cols(right)], v_s.at[0], v_r.at[2], partner)

    @pl.when(near)
    def _():
        weights(2)

    def weight_tile(q):
        total = None
        for b in range(2):
            part = dot(li2[b], vg[b, :, cols(q)], ((0,), (0,))).astype(BF).astype(F32)
            total = part if total is None else total + part
        wp[2 * q] = total[:, :COLS]
        wp[2 * q + 1] = total[:, COLS:]

    send(res_ref.at[:, mine(1 - c)], res2.at[1], p_s.at[0], p_r.at[3], partner)

    own_vg.wait()
    own_li.wait()
    got(li2.at[1], p_r.at[0])
    got(vg.at[1, :, cols(x)], v_r.at[0])
    weight_tile(x)

    got(own_p, p_r.at[1])
    got(key_p, p_r.at[2])
    slot[1] = places(own_p[...])
    @pl.when(near)
    def _():
        weights(3)

    got(vg.at[0, low, cols(left)], x_r.at[1])
    send(vg.at[0, low, cols(left)], vg.at[1, low, cols(left)], v_s.at[0], v_r.at[1], partner)
    got(vg.at[0, top, cols(right)], x_r.at[3])
    send(vg.at[0, top, cols(right)], vg.at[1, top, cols(right)], v_s.at[0], v_r.at[2], partner)

    @pl.when(near)
    def _():
        weights(4)

    across = (x + 2) % NX
    got(vg.at[0, top, cols(across)], x_r.at[4])
    send(vg.at[0, top, cols(across)], vg.at[1, top, cols(across)], v_s.at[0], v_r.at[3], partner)
    got(vg.at[0, low, cols(across)], x_r.at[5])
    send(vg.at[0, low, cols(across)], vg.at[1, low, cols(across)], v_s.at[0], v_r.at[3], partner)

    own_res.wait()
    got(res2.at[1], p_r.at[3])
    acc[...] = res2[...].astype(F32)

    @pl.when(near)
    def _():
        pltpu.make_async_copy(wsh_ref, w.at[block(y)], loc.at[3]).wait()

    @pl.when(far)
    def _():
        got(w, wz_r.at[0])

    def back_tile(q, h=None):
        start, size = (0, FEAT) if h is None else CHUNKS[h]
        for b in range(2):
            acc[b, :, start : start + size] += dot(vg[b, :, cols(q)], w[start : start + size, cols(q)], ((1,), (1,)))

    back_tile(x)
    got(vg.at[1, :, cols(left)], v_r.at[1])
    back_tile(left)
    got(vg.at[1, :, cols(right)], v_r.at[2])
    back_tile(right)
    got(vg.at[1, :, cols(across)], v_r.at[3])

    line = lax.broadcasted_iota(jnp.int32, (2 * SLOTS, 1), 0)
    keys = [jnp.broadcast_to((ref[...] + 1).astype(F32), (8, TOK)).astype(BF) for ref in (key_ref, key_p)]

    def pack(h):
        start, size = CHUNKS[h]
        back_tile(across, h)
        igb[:, :, start : start + size] = acc[:, :, start : start + size].astype(BF)
        for d in (*ORDER, 0):
            to = (y + d) % NY
            wanted = (line // SLOTS) * (NY * SLOTS) + to * SLOTS + line % SLOTS
            for b in range(2):
                pick = (wanted == slot[b]).astype(F32).astype(BF)
                picked = dot(pick, igb[b, :, start : start + size], ((1,), (0,)))
                pk[h][d, pl.ds(b * 2 * SLOTS, 2 * SLOTS)] = picked.astype(BF)
                if h == 0:
                    km[d, :, pl.ds(b * 2 * SLOTS, 2 * SLOTS)] = dot(keys[b], pick, ((1,), (1,)))
            if h < 2 and 2 <= d <= 6:
                ship(h, d)

    parts = (pl.ds(0, 2 * SLOTS), pl.ds(2 * SLOTS, 2 * SLOTS))

    def ship(h, d):
        for way in range(2):
            if (d, way) in ((2, 1), (3, 1), (5, 0), (6, 0)):
                continue
            place = d - 1 if way == 0 else d + 1
            to = at(y_=(y + place) % NY)
            if h == 0:
                send(km.at[d], kmr.at[place], m_s.at[0], m_r.at[0], to)
            src, dst = pk[h].at[d], kr[h].at[place]
            if d == 4:
                src, dst = pk[h].at[d, parts[way]], kr[h].at[place, parts[way]]
            send(src, dst, k_s.at[h], k_r.at[8 * h + place], to)

    def rows(r):
        return pl.ds(r * PART, PART)

    def hop(way, s, r, src, dst):
        number = 8 * way + 2 * s + r
        send(src, dst, c_s.at[0], c_r.at[number], up if way == 0 else down)

    def goal(way, s):
        return (z + 4 - s) % NZ if way == 0 else (z + 4 + s) % NZ

    def start(way, s, r):
        cs[way, s, rows(r)] = wp[goal(way, s), rows(r)].astype(BF)
        hop(way, s, r, cs.at[way, s, rows(r)], cr.at[way, s, rows(r)])

    def tally(rows_, marks):
        slots = rows_.shape[0]
        lane = lax.broadcasted_iota(jnp.int32, (1, slots), 1)
        named = marks[0:1, :].astype(jnp.int32)
        number = jnp.where(named > 0, named + ((lane // SLOTS) % 2) * KEYS - 1, -1)
        hit = (lax.broadcasted_iota(jnp.int32, (2 * KEYS, slots), 0) == number).astype(F32).astype(BF)
        return dot(hit, rows_, ((1,), (0,)))

    def gate(h):
        if h == 0:
            got(kmr.at[pl.ds(0, 6)], m_r.at[0])
        for way in range(2):
            own, places_ = ((1, (1, 2, 3)), (7, (7, 6, 5)))[way]
            total = tally(pk[h][own], km[own])
            for place in places_:
                if place in (3, 5):
                    got(kr[h].at[place, parts[way]], k_r.at[8 * h + place])
                    total = total + tally(kr[h][place, parts[way]], kmr[place, :, parts[way]])
                else:
                    got(kr[h].at[place], k_r.at[8 * h + place])
                    total = total + tally(kr[h][place], kmr[place])
            gt[h][way] = total.astype(BF)
            to = after if way == 0 else before
            send(gt[h].at[way], gr[h].at[way], n_s.at[h], n_r.at[2 * h + way], to)

    pack(0)
    weight_tile(left)
    weight_tile(right)
    weight_tile(across)
    for way in range(2):
        start(way, 0, way)
    for way in range(2):
        start(way, 1, 1 - way)
    pack(1)
    for s in range(1, 4):
        if s == 2:
            pack(2)
        if s == 3:
            gate(0)
            for d in ORDER[:5]:
                ship(2, d)
        for turn in range(2):
            for way in range(2):
                r = 1 - way if turn == 0 else way
                if s == 1 and r != way:
                    continue
                got(cr.at[way, s - 1, rows(r)], c_r.at[8 * way + 2 * (s - 1) + r])
                total = wp[goal(way, s), rows(r)] + cr[way, s - 1, rows(r)].astype(F32)
                if s < 3:
                    cs[way, s, rows(r)] = total.astype(BF)
                    hop(way, s, r, cs.at[way, s, rows(r)], cr.at[way, s, rows(r)])
                else:
                    cfs[way, rows(r)] = total
                    hop(way, s, r, cfs.at[way, rows(r)], cfr.at[way, rows(r)])

    def piece(place):
        return block((place % 2) * NH + place // 2)

    def tables(h):
        start, size = CHUNKS[h]
        here = pl.ds(start, size)
        table[:, here] = tally(pk[h][0], km[0])
        for way in range(2):
            got(gr[h].at[way], n_r.at[2 * h + way])
            table[:, here] += gr[h][way].astype(F32)
        tb[h][...] = table[:, here].astype(BF)
        for d in ORDER:
            to = (z + d) % NZ
            send(tb[h].at[piece(to)], zr[h].at[d], z_s.at[h], z_r.at[h], at(z_=to))

    def strip(i, h):
        start, size = CHUNKS[h]
        return pl.ds(pl.multiple_of(i * FEAT + start, 128), size)

    def finish_keys(h):
        start, size = CHUNKS[h]
        got(zr[h].at[REST], z_r.at[h])
        total = table[piece(z), pl.ds(start, size)]
        for d in ORDER:
            total = total + zr[h][d].astype(F32)
        kb[h][...] = total.astype(BF)
        here = kout.at[block(zh), strip(c, h)]
        for e in (2, 1, 3):
            send(kb[h], here, d_s.at[0], d_r.at[4 * h + e], at(z_=((zh + e) % NH) * 2 + zl))
        send(kb[h], here, e_s.at[0], e_r.at[0], partner)
        pltpu.make_async_copy(kb[h], here, loc.at[4 + h]).start()

    def pass_keys(h):
        for e in (1, 3, 2):
            here = kout.at[block((zh + NH - e) % NH), strip(c, h)]
            got(here, d_r.at[4 * h + e])
            send(here, here, e_s.at[0], e_r.at[0], partner)

    gate(1)
    tables(0)

    for r in range(2):
        for way in range(2):
            got(cfr.at[way, rows(r)], c_r.at[8 * way + 6 + r])
        total = wp[z, rows(r)] + cfr[0, rows(r)] + cfr[1, rows(r)]
        ctot[rows(r)] = total
        ws[rows(r)] = total.astype(BF)
    gate(2)
    for d in ORDER:
        to = (y + d) % NY
        send(ws.at[block(to)], yr.at[d], b_s.at[0], b_r.at[0], at(y_=to))

    finish_keys(0)
    tables(1)
    tables(2)

    got(yr.at[REST], b_r.at[0])
    total = ctot[block(y), :]
    for d in ORDER:
        total = total + yr[d].astype(F32)
    wf[...] = total

    def heads(i):
        return pl.ds(pl.multiple_of(i * COLS, COLS), COLS)

    for e in (2, 1, 3):
        send(wf, wout.at[:, heads(z)], f_s.at[0], f_r.at[z], at(z_=((zh + e) % NH) * 2 + c))

    @pl.when(far)
    def _():
        send(wf, wout.at[:, heads(z)], f_s.at[0], f_r.at[z], at(z_=zh * 2 + c))

    @pl.when(near)
    def _():
        pltpu.make_async_copy(wf, wout.at[:, heads(z)], loc.at[7]).start()
        send(wf, wout.at[:, heads(z)], g_s.at[0], g_r.at[0], partner)

    finish_keys(1)
    pass_keys(0)
    finish_keys(2)
    pass_keys(1)
    pass_keys(2)

    @pl.when(near)
    def _():
        for d in (1, 7, 2, 6, 3, 5, 4):
            here = wout.at[:, heads((z + d) % NZ)]
            got(here, f_r.at[(z + d) % NZ])
            send(here, here, g_s.at[0], g_r.at[0], partner)

    @pl.when(far)
    def _():
        got(wout, g_r.at[0])

    got(kout.at[:, mine(1 - c)], e_r.at[0])
    for h in range(3):
        got(kb[h], loc.at[4 + h])

    got(vg.at[0, :, pl.ds(0, 3 * HEADS)], x_s.at[0])
    got(vg.at[0], v_s.at[0])
    got(li2, p_s.at[0])
    got(own_p, p_s.at[1])
    got(key_p, p_s.at[2])
    got(vg.at[:, pl.ds(0, 288)], c_s.at[0])
    for h in range(3):
        got(kr[h].at[pl.ds(0, 5)], k_s.at[h])
        got(gr[h], n_s.at[h])
        got(zr[h].at[REST], z_s.at[h])
    got(kmr.at[pl.ds(0, 6)], m_s.at[0])
    got(yr.at[REST], b_s.at[0])
    got(w.at[pl.ds(0, 48)], d_s.at[0])
    got(w.at[pl.ds(0, 64)], e_s.at[0])

    @pl.when(near)
    def _():
        got(w.at[pl.ds(0, 448)], wy_s.at[0])
        got(w, wz_s.at[0])
        got(w.at[pl.ds(0, 48)], f_s.at[0])
        got(w.at[pl.ds(0, 128)], g_s.at[0])
        got(wf, loc.at[7])

    @pl.when(far)
    def _():
        got(w.at[pl.ds(0, 64)], f_s.at[0])


def body(layer_input, value_grad, residual_grad, value_weight, owner, key_row):
    dma = pltpu.SemaphoreType.DMA
    vmem = pl.BlockSpec(memory_space=pltpu.VMEM)
    hbm = pl.BlockSpec(memory_space=pl.ANY)
    scratch = [
        pltpu.VMEM((2, TOK, WIDTH), BF),
        pltpu.VMEM((2, TOK, FEAT), BF),
        pltpu.VMEM((2, TOK, FEAT), BF),
        pltpu.VMEM((1, TOK), jnp.int32),
        pltpu.VMEM((1, TOK), jnp.int32),
        pltpu.VMEM((FEAT, WIDTH), BF),
        pltpu.VMEM((NZ, FEAT, COLS), F32),
        pltpu.VMEM((2, 3, FEAT, COLS), BF),
        pltpu.VMEM((2, 3, FEAT, COLS), BF),
        pltpu.VMEM((2, FEAT, COLS), F32),
        pltpu.VMEM((2, FEAT, COLS), F32),
        pltpu.VMEM((FEAT, COLS), F32),
        pltpu.VMEM((FEAT, COLS), BF),
        pltpu.VMEM((NY, ROWS, COLS), BF),
        pltpu.VMEM((ROWS, COLS), F32),
        pltpu.VMEM((2, TOK, FEAT), F32),
        pltpu.VMEM((2, TOK, FEAT), BF),
    ]
    widths = [size for _, size in CHUNKS]
    scratch += [pltpu.VMEM((NY, 4 * SLOTS, size), BF) for size in widths]
    scratch += [pltpu.VMEM((NY, 8, 4 * SLOTS), F32)]
    scratch += [pltpu.VMEM((NY, 4 * SLOTS, size), BF) for size in widths]
    scratch += [pltpu.VMEM((NY, 8, 4 * SLOTS), F32), pltpu.VMEM((2 * KEYS, FEAT), F32)]
    scratch += [pltpu.VMEM((2 * KEYS, size), BF) for size in widths]
    scratch += [pltpu.VMEM((NZ, ROWS, size), BF) for size in widths]
    scratch += [pltpu.VMEM((ROWS, size), BF) for size in widths]
    scratch += [pltpu.VMEM((2, 2 * KEYS, size), BF) for size in (*widths, *widths)]
    scratch += [dma((8,))]
    for sent, received in ((3, 4), (1, 6), (1, 4), (1, 16), (1, 1), (1, 16), (3, 24), (1, 1), (1, 1), (3, 3), (1, 12), (1, 1)):
        scratch += [dma((sent,)), dma((received,))]
    scratch += [dma((1,)), dma((8,)), dma((1,)), dma((1,)), dma((3,)), dma((6,))]
    weight_grad, key_grad = pl.pallas_call(
        kernel,
        out_shape=(
            pltpu.VMEM((ROWS, WIDTH), F32),
            pltpu.VMEM((KEYS, 2 * FEAT), BF),
        ),
        in_specs=[hbm, hbm, hbm, hbm, vmem, vmem],
        out_specs=(vmem, vmem),
        scratch_shapes=scratch,
        compiler_params=pltpu.CompilerParams(
            collective_id=0, has_side_effects=True, vmem_limit_bytes=60 * 1024 * 1024
        ),
    )(layer_input, value_grad, residual_grad, value_weight, owner.reshape(1, TOK), key_row.reshape(1, TOK))
    return weight_grad, key_grad.astype(F32)


def solution(mesh):
    return jax.shard_map(
        body,
        mesh=mesh,
        in_specs=(
            P(("dp", "fsdp"), "tp"),
            P(("dp", "fsdp"), "tp"),
            P(("dp", "fsdp"), "tp"),
            P(("tp", "fsdp"), None),
            P(("dp", "fsdp"), None),
            P(("dp", "fsdp")),
        ),
        out_specs=(P(("tp", "fsdp"), None), P("fsdp", "tp")),
        check_vma=False,
    )
```

```python
import jax
import jax.numpy as jnp
from jax import lax
from jax.experimental import pallas as pl
from jax.experimental.pallas import tpu as pltpu
from jax.sharding import PartitionSpec as P

MESH = pl.DeviceIdType.MESH
BF, F32 = jnp.bfloat16, jnp.float32
NX, NY, NZ, NH = 4, 8, 8, 4
TOK, FEAT, HEADS, WIDTH = 512, 512, 512, 2048
SLOTS, KEYS, ROWS, COLS = 64, 256, 64, 256
HALF = TOK // 2
PART = FEAT // 2
ORDER = (4, 3, 5, 2, 6, 1, 7)
CHUNKS = ((0, 256), (256, 128), (384, 128))
REST = pl.ds(1, NY - 1)


def dot(a, b, dims):
    return lax.dot_general(a, b, (dims, ((), ())), preferred_element_type=F32)


def kernel(
    li_ref, vgr_ref, res_ref, wsh_ref, own_ref, key_ref,
    wout, kout,
    vg, li2, res2, own_p, key_p, w, wp, cr, cs, cfs, cfr, ctot, ws, yr, wf, acc, igb, pk0, pk1, pk2, km, kr0, kr1, kr2, kmr, table, tb0, tb1, tb2, zr0, zr1, zr2, kb0, kb1, kb2, gt0, gt1, gt2, gr0, gr1, gr2,
    loc, p_s, p_r, x_s, x_r, v_s, v_r, wy_s, wy_r, wz_s, wz_r,
    c_s, c_r, k_s, k_r, m_s, m_r, b_s, b_r, z_s, z_r, d_s, d_r, e_s, e_r, f_s, f_r, g_s, g_r, n_s, n_r,
):
    dp, fs, x = lax.axis_index("dp"), lax.axis_index("fsdp"), lax.axis_index("tp")
    zh, c, zl, y = dp // 2, dp % 2, fs // NY, fs % NY
    z = zh * 2 + zl
    near = zl == c
    far = zl != c

    def at(x_=x, y_=y, z_=z, c_=c):
        return ((z_ // 2) * 2 + c_, (z_ % 2) * NY + y_, x_)

    partner = at(c_=1 - c)
    right, left = (x + 1) % NX, (x + NX - 1) % NX
    pk, kr, tb = (pk0, pk1, pk2), (kr0, kr1, kr2), (tb0, tb1, tb2)
    zr, kb, gt, gr = (zr0, zr1, zr2), (kb0, kb1, kb2), (gt0, gt1, gt2), (gr0, gr1, gr2)

    def send(src, dst, ss, rs, to):
        pltpu.make_async_remote_copy(
            src_ref=src, dst_ref=dst, send_sem=ss, recv_sem=rs, device_id=to, device_id_type=MESH
        ).start()

    def got(dst, rs):
        pltpu.make_async_copy(dst, dst, rs).wait()

    def cols(i):
        return pl.ds(pl.multiple_of(i * HEADS, HEADS), HEADS)

    def mine(i):
        return pl.ds(pl.multiple_of(i * FEAT, FEAT), FEAT)

    def half(i, h):
        return pl.ds(pl.multiple_of(i * ROWS + h * 32, 32), 32)

    def block(i):
        return pl.ds(pl.multiple_of(i * ROWS, ROWS), ROWS)

    barrier = pltpu.get_barrier_semaphore()
    peers = [partner, at(x_=right), at(x_=left)]
    peers += [at(y_=(y + d) % NY) for d in range(1, NY)] + [at(z_=(z + d) % NZ) for d in range(1, NZ)]
    for peer in peers:
        pl.semaphore_signal(barrier, inc=1, device_id=peer, device_id_type=MESH)

    own_vg = pltpu.make_async_copy(vgr_ref, vg.at[0, :, cols(x)], loc.at[0])
    own_vg.start()
    own_li = pltpu.make_async_copy(li_ref.at[:, mine(c)], li2.at[0], loc.at[1])
    own_li.start()
    own_res = pltpu.make_async_copy(res_ref.at[:, mine(c)], res2.at[0], loc.at[2])
    own_res.start()

    @pl.when(near)
    def _():
        pltpu.make_async_copy(wsh_ref, w.at[block(y)], loc.at[3]).start()

    pl.semaphore_wait(barrier, len(peers))

    up, down = at(z_=(z + 1) % NZ), at(z_=(z + NZ - 1) % NZ)
    after, before = at(y_=(y + 1) % NY), at(y_=(y + NY - 1) % NY)
    first, second = pl.ds(0, 32), pl.ds(32, 32)

    @pl.when(near)
    def _():
        for h, rows in enumerate((first, second)):
            send(wsh_ref.at[rows], w.at[half(y, h)], wy_s.at[0], wy_r.at[h], after)
            send(wsh_ref.at[rows], w.at[half(y, h)], wy_s.at[0], wy_r.at[8 + h], before)
        send(wsh_ref.at[first], w.at[half(y, 0)], wz_s.at[0], wz_r.at[0], up)
        send(wsh_ref.at[second], w.at[half(y, 1)], wz_s.at[0], wz_r.at[0], down)

    top, low = pl.ds(0, HALF), pl.ds(HALF, HALF)
    send(vgr_ref.at[top], vg.at[0, top, cols(x)], x_s.at[0], x_r.at[0], at(x_=right))
    send(vgr_ref.at[low], vg.at[0, low, cols(x)], x_s.at[0], x_r.at[2], at(x_=left))
    send(vgr_ref.at[low], vg.at[0, low, cols(x)], x_s.at[0], x_r.at[1], at(x_=right))
    send(vgr_ref.at[top], vg.at[0, top, cols(x)], x_s.at[0], x_r.at[3], at(x_=left))
    send(own_ref, own_p, p_s.at[1], p_r.at[1], partner)
    send(key_ref, key_p, p_s.at[2], p_r.at[2], partner)

    def weights(k):
        plus, minus = (y + NY - k) % NY, (y + k) % NY
        for h in range(2):
            for base, shard, onward, side, keeps in ((0, plus, after, down, 0), (8, minus, before, up, 1)):
                if k == 4 and h != keeps:
                    continue
                here = w.at[half(shard, h)]
                got(here, wy_r.at[base + 2 * (k - 1) + h])
                if k < 3 or (k == 3 and h == keeps):
                    send(here, here, wy_s.at[0], wy_r.at[base + 2 * k + h], onward)
                if k < 4:
                    send(here, here, wz_s.at[0], wz_r.at[0], side)
                else:
                    send(here, here, wz_s.at[0], wz_r.at[0], up if base == 0 else down)

    def places(owner):
        hot = (lax.broadcasted_iota(jnp.int32, (16, TOK), 0) == owner).astype(F32)
        order = lax.broadcasted_iota(jnp.int32, (TOK, TOK), 0) <= lax.broadcasted_iota(jnp.int32, (TOK, TOK), 1)
        count = dot(hot.astype(BF), order.astype(F32).astype(BF), ((1,), (0,)))
        rank = jnp.sum(count * hot, axis=0, keepdims=True) - 1.0
        return owner * SLOTS + rank.astype(jnp.int32)

    slot = [places(own_ref[...]), None]

    @pl.when(near)
    def _():
        weights(1)

    send(vgr_ref, vg.at[1, :, cols(x)], v_s.at[0], v_r.at[0], partner)
    send(li_ref.at[:, mine(1 - c)], li2.at[1], p_s.at[0], p_r.at[0], partner)

    got(vg.at[0, top, cols(left)], x_r.at[0])
    send(vg.at[0, top, cols(left)], vg.at[0, top, cols(left)], x_s.at[0], x_r.at[4], at(x_=right))
    send(vg.at[0, top, cols(left)], vg.at[1, top, cols(left)], v_s.at[0], v_r.at[1], partner)
    got(vg.at[0, low, cols(right)], x_r.at[2])
    send(vg.at[0, low, cols(right)], vg.at[0, low, cols(right)], x_s.at[0], x_r.at[5], at(x_=left))
    send(vg.at[0, low, cols(right)], vg.at[1, low, cols(right)], v_s.at[0], v_r.at[2], partner)

    @pl.when(near)
    def _():
        weights(2)

    def weight_tile(q):
        total = None
        for b in range(2):
            part = dot(li2[b], vg[b, :, cols(q)], ((0,), (0,))).astype(BF).astype(F32)
            total = part if total is None else total + part
        wp[2 * q] = total[:, :COLS]
        wp[2 * q + 1] = total[:, COLS:]

    send(res_ref.at[:, mine(1 - c)], res2.at[1], p_s.at[0], p_r.at[3], partner)

    own_vg.wait()
    own_li.wait()
    got(li2.at[1], p_r.at[0])
    got(vg.at[1, :, cols(x)], v_r.at[0])
    weight_tile(x)

    got(own_p, p_r.at[1])
    got(key_p, p_r.at[2])
    slot[1] = places(own_p[...])
    @pl.when(near)
    def _():
        weights(3)

    got(vg.at[0, low, cols(left)], x_r.at[1])
    send(vg.at[0, low, cols(left)], vg.at[1, low, cols(left)], v_s.at[0], v_r.at[1], partner)
    got(vg.at[0, top, cols(right)], x_r.at[3])
    send(vg.at[0, top, cols(right)], vg.at[1, top, cols(right)], v_s.at[0], v_r.at[2], partner)

    @pl.when(near)
    def _():
        weights(4)

    got(vg.at[1, :, cols(left)], v_r.at[1])
    weight_tile(left)
    got(vg.at[1, :, cols(right)], v_r.at[2])
    weight_tile(right)

    across = (x + 2) % NX
    got(vg.at[0, top, cols(across)], x_r.at[4])
    send(vg.at[0, top, cols(across)], vg.at[1, top, cols(across)], v_s.at[0], v_r.at[3], partner)
    got(vg.at[0, low, cols(across)], x_r.at[5])
    send(vg.at[0, low, cols(across)], vg.at[1, low, cols(across)], v_s.at[0], v_r.at[3], partner)

    own_res.wait()
    got(res2.at[1], p_r.at[3])
    acc[...] = res2[...].astype(F32)

    @pl.when(near)
    def _():
        pltpu.make_async_copy(wsh_ref, w.at[block(y)], loc.at[3]).wait()

    @pl.when(far)
    def _():
        got(w, wz_r.at[0])

    def back_tile(q, h=None):
        start, size = (0, FEAT) if h is None else CHUNKS[h]
        for b in range(2):
            acc[b, :, start : start + size] += dot(vg[b, :, cols(q)], w[start : start + size, cols(q)], ((1,), (1,)))

    back_tile(x)
    back_tile(left)
    back_tile(right)
    got(vg.at[1, :, cols(across)], v_r.at[3])

    line = lax.broadcasted_iota(jnp.int32, (2 * SLOTS, 1), 0)
    keys = [jnp.broadcast_to((ref[...] + 1).astype(F32), (8, TOK)).astype(BF) for ref in (key_ref, key_p)]

    def pack(h):
        start, size = CHUNKS[h]
        back_tile(across, h)
        igb[:, :, start : start + size] = acc[:, :, start : start + size].astype(BF)
        for d in (*ORDER, 0):
            to = (y + d) % NY
            wanted = (line // SLOTS) * (NY * SLOTS) + to * SLOTS + line % SLOTS
            for b in range(2):
                pick = (wanted == slot[b]).astype(F32).astype(BF)
                picked = dot(pick, igb[b, :, start : start + size], ((1,), (0,)))
                pk[h][d, pl.ds(b * 2 * SLOTS, 2 * SLOTS)] = picked.astype(BF)
                if h == 0:
                    km[d, :, pl.ds(b * 2 * SLOTS, 2 * SLOTS)] = dot(keys[b], pick, ((1,), (1,)))
            if h < 2 and 2 <= d <= 6:
                ship(h, d)

    parts = (pl.ds(0, 2 * SLOTS), pl.ds(2 * SLOTS, 2 * SLOTS))

    def ship(h, d):
        for way in range(2):
            if (d, way) in ((2, 1), (3, 1), (5, 0), (6, 0)):
                continue
            place = d - 1 if way == 0 else d + 1
            to = at(y_=(y + place) % NY)
            if h == 0:
                send(km.at[d], kmr.at[place], m_s.at[0], m_r.at[0], to)
            src, dst = pk[h].at[d], kr[h].at[place]
            if d == 4:
                src, dst = pk[h].at[d, parts[way]], kr[h].at[place, parts[way]]
            send(src, dst, k_s.at[h], k_r.at[8 * h + place], to)

    def rows(r):
        return pl.ds(r * PART, PART)

    def hop(way, s, r, src, dst):
        number = 8 * way + 2 * s + r
        send(src, dst, c_s.at[0], c_r.at[number], up if way == 0 else down)

    def goal(way, s):
        return (z + 4 - s) % NZ if way == 0 else (z + 4 + s) % NZ

    def start(way, s, r):
        cs[way, s, rows(r)] = wp[goal(way, s), rows(r)].astype(BF)
        hop(way, s, r, cs.at[way, s, rows(r)], cr.at[way, s, rows(r)])

    def tally(rows_, marks):
        slots = rows_.shape[0]
        lane = lax.broadcasted_iota(jnp.int32, (1, slots), 1)
        named = marks[0:1, :].astype(jnp.int32)
        number = jnp.where(named > 0, named + ((lane // SLOTS) % 2) * KEYS - 1, -1)
        hit = (lax.broadcasted_iota(jnp.int32, (2 * KEYS, slots), 0) == number).astype(F32).astype(BF)
        return dot(hit, rows_, ((1,), (0,)))

    def gate(h):
        if h == 0:
            got(kmr.at[pl.ds(0, 6)], m_r.at[0])
        for way in range(2):
            own, places_ = ((1, (1, 2, 3)), (7, (7, 6, 5)))[way]
            total = tally(pk[h][own], km[own])
            for place in places_:
                if place in (3, 5):
                    got(kr[h].at[place, parts[way]], k_r.at[8 * h + place])
                    total = total + tally(kr[h][place, parts[way]], kmr[place, :, parts[way]])
                else:
                    got(kr[h].at[place], k_r.at[8 * h + place])
                    total = total + tally(kr[h][place], kmr[place])
            gt[h][way] = total.astype(BF)
            to = after if way == 0 else before
            send(gt[h].at[way], gr[h].at[way], n_s.at[h], n_r.at[2 * h + way], to)

    weight_tile(across)
    for way in range(2):
        start(way, 0, way)
    for way in range(2):
        start(way, 1, 1 - way)
    pack(0)
    pack(1)
    for s in range(1, 4):
        if s == 2:
            pack(2)
        if s == 3:
            gate(0)
            for d in ORDER[:5]:
                ship(2, d)
        for turn in range(2):
            for way in range(2):
                r = 1 - way if turn == 0 else way
                if s == 1 and r != way:
                    continue
                got(cr.at[way, s - 1, rows(r)], c_r.at[8 * way + 2 * (s - 1) + r])
                total = wp[goal(way, s), rows(r)] + cr[way, s - 1, rows(r)].astype(F32)
                if s < 3:
                    cs[way, s, rows(r)] = total.astype(BF)
                    hop(way, s, r, cs.at[way, s, rows(r)], cr.at[way, s, rows(r)])
                else:
                    cfs[way, rows(r)] = total
                    hop(way, s, r, cfs.at[way, rows(r)], cfr.at[way, rows(r)])

    def piece(place):
        return block((place % 2) * NH + place // 2)

    def tables(h):
        start, size = CHUNKS[h]
        here = pl.ds(start, size)
        table[:, here] = tally(pk[h][0], km[0])
        for way in range(2):
            got(gr[h].at[way], n_r.at[2 * h + way])
            table[:, here] += gr[h][way].astype(F32)
        tb[h][...] = table[:, here].astype(BF)
        for d in ORDER:
            to = (z + d) % NZ
            send(tb[h].at[piece(to)], zr[h].at[d], z_s.at[h], z_r.at[h], at(z_=to))

    def strip(i, h):
        start, size = CHUNKS[h]
        return pl.ds(pl.multiple_of(i * FEAT + start, 128), size)

    def finish_keys(h):
        start, size = CHUNKS[h]
        got(zr[h].at[REST], z_r.at[h])
        total = table[piece(z), pl.ds(start, size)]
        for d in ORDER:
            total = total + zr[h][d].astype(F32)
        kb[h][...] = total.astype(BF)
        here = kout.at[block(zh), strip(c, h)]
        for e in (2, 1, 3):
            send(kb[h], here, d_s.at[0], d_r.at[4 * h + e], at(z_=((zh + e) % NH) * 2 + zl))
        send(kb[h], here, e_s.at[0], e_r.at[0], partner)
        pltpu.make_async_copy(kb[h], here, loc.at[4 + h]).start()

    def pass_keys(h):
        for e in (1, 3, 2):
            here = kout.at[block((zh + NH - e) % NH), strip(c, h)]
            got(here, d_r.at[4 * h + e])
            send(here, here, e_s.at[0], e_r.at[0], partner)

    gate(1)
    tables(0)

    for r in range(2):
        for way in range(2):
            got(cfr.at[way, rows(r)], c_r.at[8 * way + 6 + r])
        total = wp[z, rows(r)] + cfr[0, rows(r)] + cfr[1, rows(r)]
        ctot[rows(r)] = total
        ws[rows(r)] = total.astype(BF)
    gate(2)
    for d in ORDER:
        to = (y + d) % NY
        send(ws.at[block(to)], yr.at[d], b_s.at[0], b_r.at[0], at(y_=to))

    finish_keys(0)
    tables(1)
    tables(2)

    got(yr.at[REST], b_r.at[0])
    total = ctot[block(y), :]
    for d in ORDER:
        total = total + yr[d].astype(F32)
    wf[...] = total

    def heads(i):
        return pl.ds(pl.multiple_of(i * COLS, COLS), COLS)

    for e in (2, 1, 3):
        send(wf, wout.at[:, heads(z)], f_s.at[0], f_r.at[z], at(z_=((zh + e) % NH) * 2 + c))

    @pl.when(far)
    def _():
        send(wf, wout.at[:, heads(z)], f_s.at[0], f_r.at[z], at(z_=zh * 2 + c))

    @pl.when(near)
    def _():
        pltpu.make_async_copy(wf, wout.at[:, heads(z)], loc.at[7]).start()
        send(wf, wout.at[:, heads(z)], g_s.at[0], g_r.at[0], partner)

    finish_keys(1)
    pass_keys(0)
    finish_keys(2)
    pass_keys(1)
    pass_keys(2)

    @pl.when(near)
    def _():
        for d in (1, 7, 2, 6, 3, 5, 4):
            here = wout.at[:, heads((z + d) % NZ)]
            got(here, f_r.at[(z + d) % NZ])
            send(here, here, g_s.at[0], g_r.at[0], partner)

    @pl.when(far)
    def _():
        got(wout, g_r.at[0])

    got(kout.at[:, mine(1 - c)], e_r.at[0])
    for h in range(3):
        got(kb[h], loc.at[4 + h])

    got(vg.at[0, :, pl.ds(0, 3 * HEADS)], x_s.at[0])
    got(vg.at[0], v_s.at[0])
    got(li2, p_s.at[0])
    got(own_p, p_s.at[1])
    got(key_p, p_s.at[2])
    got(vg.at[:, pl.ds(0, 288)], c_s.at[0])
    for h in range(3):
        got(kr[h].at[pl.ds(0, 5)], k_s.at[h])
        got(gr[h], n_s.at[h])
        got(zr[h].at[REST], z_s.at[h])
    got(kmr.at[pl.ds(0, 6)], m_s.at[0])
    got(yr.at[REST], b_s.at[0])
    got(w.at[pl.ds(0, 48)], d_s.at[0])
    got(w.at[pl.ds(0, 64)], e_s.at[0])

    @pl.when(near)
    def _():
        got(w.at[pl.ds(0, 448)], wy_s.at[0])
        got(w, wz_s.at[0])
        got(w.at[pl.ds(0, 48)], f_s.at[0])
        got(w.at[pl.ds(0, 128)], g_s.at[0])
        got(wf, loc.at[7])

    @pl.when(far)
    def _():
        got(w.at[pl.ds(0, 64)], f_s.at[0])


def body(layer_input, value_grad, residual_grad, value_weight, owner, key_row):
    dma = pltpu.SemaphoreType.DMA
    vmem = pl.BlockSpec(memory_space=pltpu.VMEM)
    hbm = pl.BlockSpec(memory_space=pl.ANY)
    scratch = [
        pltpu.VMEM((2, TOK, WIDTH), BF),
        pltpu.VMEM((2, TOK, FEAT), BF),
        pltpu.VMEM((2, TOK, FEAT), BF),
        pltpu.VMEM((1, TOK), jnp.int32),
        pltpu.VMEM((1, TOK), jnp.int32),
        pltpu.VMEM((FEAT, WIDTH), BF),
        pltpu.VMEM((NZ, FEAT, COLS), F32),
        pltpu.VMEM((2, 3, FEAT, COLS), BF),
        pltpu.VMEM((2, 3, FEAT, COLS), BF),
        pltpu.VMEM((2, FEAT, COLS), F32),
        pltpu.VMEM((2, FEAT, COLS), F32),
        pltpu.VMEM((FEAT, COLS), F32),
        pltpu.VMEM((FEAT, COLS), BF),
        pltpu.VMEM((NY, ROWS, COLS), BF),
        pltpu.VMEM((ROWS, COLS), F32),
        pltpu.VMEM((2, TOK, FEAT), F32),
        pltpu.VMEM((2, TOK, FEAT), BF),
    ]
    widths = [size for _, size in CHUNKS]
    scratch += [pltpu.VMEM((NY, 4 * SLOTS, size), BF) for size in widths]
    scratch += [pltpu.VMEM((NY, 8, 4 * SLOTS), F32)]
    scratch += [pltpu.VMEM((NY, 4 * SLOTS, size), BF) for size in widths]
    scratch += [pltpu.VMEM((NY, 8, 4 * SLOTS), F32), pltpu.VMEM((2 * KEYS, FEAT), F32)]
    scratch += [pltpu.VMEM((2 * KEYS, size), BF) for size in widths]
    scratch += [pltpu.VMEM((NZ, ROWS, size), BF) for size in widths]
    scratch += [pltpu.VMEM((ROWS, size), BF) for size in widths]
    scratch += [pltpu.VMEM((2, 2 * KEYS, size), BF) for size in (*widths, *widths)]
    scratch += [dma((8,))]
    for sent, received in ((3, 4), (1, 6), (1, 4), (1, 16), (1, 1), (1, 16), (3, 24), (1, 1), (1, 1), (3, 3), (1, 12), (1, 1)):
        scratch += [dma((sent,)), dma((received,))]
    scratch += [dma((1,)), dma((8,)), dma((1,)), dma((1,)), dma((3,)), dma((6,))]
    weight_grad, key_grad = pl.pallas_call(
        kernel,
        out_shape=(
            pltpu.VMEM((ROWS, WIDTH), F32),
            pltpu.VMEM((KEYS, 2 * FEAT), BF),
        ),
        in_specs=[hbm, hbm, hbm, hbm, vmem, vmem],
        out_specs=(vmem, vmem),
        scratch_shapes=scratch,
        compiler_params=pltpu.CompilerParams(
            collective_id=0, has_side_effects=True, vmem_limit_bytes=60 * 1024 * 1024
        ),
    )(layer_input, value_grad, residual_grad, value_weight, owner.reshape(1, TOK), key_row.reshape(1, TOK))
    return weight_grad, key_grad.astype(F32)


def solution(mesh):
    return jax.shard_map(
        body,
        mesh=mesh,
        in_specs=(
            P(("dp", "fsdp"), "tp"),
            P(("dp", "fsdp"), "tp"),
            P(("dp", "fsdp"), "tp"),
            P(("tp", "fsdp"), None),
            P(("dp", "fsdp"), None),
            P(("dp", "fsdp")),
        ),
        out_specs=(P(("tp", "fsdp"), None), P("fsdp", "tp")),
        check_vma=False,
    )
```
